512 devices in a mesh: plane: 64 (over y, z), depth: 8 (over x, core).
Axes of the slice: x: 4, y: 8, z: 8, core: 2. Of those that a mesh axis runs over, the one named last changes fastest.
Arguments:
- volume: float32 [256, 512, 1024], P('plane', None, 'depth'), may hold values from -6 to 6
- resample: bfloat16 [512, 512], replicated, may hold values from 0 to 1, as said below
- transfer: float32 [16, 4], replicated, may hold values from 0.2 to 2
- light: float32 [3], replicated, may hold values from -4 to 4
- ray_bounds: int32 [2, 256, 512], replicated, may hold values from 0 to 1024, as said below
Outputs:
- frame: float32 [4, 256, 512], P(None, 'plane', 'depth')
The draws below stay inside these ranges and needn't reach their ends.
Inputs may be any that keep to these rules, and one draw needn't show every extreme that they name: ray_bounds[0] < ray_bounds[1] for every pixel. `resample`: row v has nonzero entries only in columns v - 1, v and v + 1.
All inputs are finite; a program needn't handle non-finite values.
Results may differ from the reference program's by a relative error of at most 0.0003.
Values sent between devices are 32-bit elements; how exact they have to be, the bound alone decides.
No kernel may reach another device: no remote copies, remote signals or barrier semaphores. Data moves between devices by JAX's collectives and lax.ppermute only.
A program may use at most 64 MiB of HBM per device.

```python
import math
import jax
import jax.numpy as jnp
from jax import lax

CX = 4
NY = 512
CZ = 128
KNOTS = 16
NX = 256
NZ = 1024


def draw_resample(key, part):
    key_diag = jax.random.fold_in(key, 11)
    key_side = jax.random.fold_in(key, 12)
    diagonal = jax.random.uniform(key_diag, (NY,), jnp.float32, 0.55, 0.8)
    sides = jax.random.uniform(key_side, (2, NY), jnp.float32, 0.1, 0.25)
    rows = jnp.arange(NY, dtype=jnp.int32)[:, None]
    columns = jnp.arange(NY, dtype=jnp.int32)[None, :]
    matrix = diagonal[:, None] * (columns == rows).astype(jnp.float32)
    matrix = matrix + sides[0][:, None] * (columns == rows - 1).astype(jnp.float32)
    matrix = matrix + sides[1][:, None] * (columns == rows + 1).astype(jnp.float32)
    return matrix.astype(jnp.bfloat16)


def draw_ray_bounds(key, part):
    key_first = jax.random.fold_in(key, 21)
    key_last = jax.random.fold_in(key, 22)
    first = jax.random.randint(key_first, (NX, NY), 0, NZ // 2, dtype=jnp.int32)
    last = NZ - jax.random.randint(key_last, (NX, NY), 0, NZ // 2, dtype=jnp.int32)
    first = first.at[0, 0].set(0)
    last = last.at[0, 0].set(NZ)
    return jnp.stack([first, last]).astype(jnp.int32)


def levels(key, dims, shards, low, largest):
    loudness = 1.0
    for position, blocks in shards:
        heights = jax.random.uniform(jax.random.fold_in(jax.random.fold_in(key, 6), position), (blocks,), jnp.float32, low / len(shards), largest / len(shards))
        loudness = loudness * jnp.repeat(jnp.exp(heights), dims[position] // blocks).reshape((-1,) + (1,) * (len(dims) - 1 - position))
    return loudness


def gaussian(own_key, dims, scale, reach, split=(), kind=jnp.bfloat16):
    array = scale * jax.random.normal(own_key, dims, jnp.float32)
    if split:
        array = array * levels(own_key, dims, split, -0.22, 0.18)
    return jnp.clip(array, -reach, reach).astype(kind)


def setup_inputs(seed: int = 0) -> dict:
    streams_of = jax.random.split(jax.random.key(seed), 6)
    volume = gaussian(streams_of[0], (NX, NY, NZ), 1.0, 6.0, ((0, 64), (2, 8)), jnp.float32)
    resample = draw_resample(jax.random.fold_in(streams_of[5], 71), 0)
    transfer = jnp.clip(jnp.exp(jax.random.uniform(streams_of[2], (KNOTS, 4), jnp.float32, math.log(0.2), math.log(2.0))), 0.2, 2.0)
    light = gaussian(streams_of[3], (3,), 1.0, 4.0, (), jnp.float32)
    ray_bounds = draw_ray_bounds(jax.random.fold_in(streams_of[5], 71), 0)
    return dict(volume=volume, resample=resample, transfer=transfer, light=light, ray_bounds=ray_bounds)


def central(field, axis):
    widths = [(1, 1) if dim == axis else (0, 0) for dim in range(3)]
    padded = jnp.pad(field, widths)
    size = field.shape[axis]
    upper = lax.slice_in_dim(padded, 2, size + 2, axis=axis)
    lower = lax.slice_in_dim(padded, 0, size, axis=axis)
    return (upper - lower) * 0.5

def shade(density, grad_x, grad_y, grad_z, transfer, light):
    scaled = jnp.clip((density + 2.5) / 5.0, 0.0, 1.0) * (transfer.shape[0] - 1)
    sigma = jnp.zeros_like(density)
    red = jnp.zeros_like(density)
    green = jnp.zeros_like(density)
    blue = jnp.zeros_like(density)
    for knot in range(transfer.shape[0]):
        hat = jnp.maximum(0.0, 1.0 - jnp.abs(scaled - knot))
        sigma = sigma + hat * transfer[knot, 3]
        red = red + hat * transfer[knot, 0]
        green = green + hat * transfer[knot, 1]
        blue = blue + hat * transfer[knot, 2]
    lit = jnp.abs(grad_x * light[0] + grad_y * light[1] + grad_z * light[2])
    lit = 0.3 + 0.7 * lit / jnp.sqrt(grad_x * grad_x + grad_y * grad_y + grad_z * grad_z + 1.0)
    return (sigma, red * lit, green * lit, blue * lit)

def reference(volume, resample, transfer, light, ray_bounds):
    fields = jnp.stack([volume.astype(jnp.bfloat16), central(volume, 0).astype(jnp.bfloat16), central(volume, 1).astype(jnp.bfloat16), central(volume, 2).astype(jnp.bfloat16)])
    group = CZ // CX
    row_block = NY // 8
    step_size = 2.0 / NZ

    def render(row_start):
        weights = lax.dynamic_slice_in_dim(resample, row_start, row_block, 0)
        samples = lax.dot_general(weights, fields, (((1,), (2,)), ((), ())), preferred_element_type=jnp.float32)
        sigma, red, green, blue = shade(samples[:, 0], samples[:, 1], samples[:, 2], samples[:, 3], transfer, light)
        channels = jnp.stack([sigma, red, green, blue])
        pieces = []
        for offset in range(NZ // group):
            piece = channels[:, :, :, offset * group:(offset + 1) * group]
            piece = jnp.pad(piece, ((0, 0), (0, 0), (offset, 0), (0, 0)))[:, :, :NX]
            pieces.append(piece)
        sheared = jnp.concatenate(pieces, axis=3)
        first = lax.dynamic_slice_in_dim(ray_bounds[0], row_start, row_block, 1).T
        last = lax.dynamic_slice_in_dim(ray_bounds[1], row_start, row_block, 1).T
        sample_index = jnp.arange(NZ, dtype=jnp.int32)
        inside = (sample_index >= first[:, :, None]) & (sample_index < last[:, :, None])
        tau = step_size * sheared[0] * inside.astype(jnp.float32)
        before = jnp.cumsum(tau, axis=2) - tau
        weight = jnp.exp(-before) * (1.0 - jnp.exp(-tau))
        color = lax.optimization_barrier(jnp.sum(weight[None] * sheared[1:], axis=3))
        opacity = 1.0 - jnp.exp(-lax.optimization_barrier(jnp.sum(tau, axis=2)))
        return jnp.concatenate([color, opacity[None]], axis=0)
    starts = jnp.arange(0, NY, row_block, dtype=jnp.int32)
    blocks = lax.map(render, starts)
    return blocks.transpose(1, 3, 0, 2).reshape(4, NX, NY)
```

```python
import functools
import math

import jax
import jax.numpy as jnp
from jax import lax
from jax.experimental import pallas as pl
from jax.experimental.pallas import tpu as pltpu
from jax.sharding import PartitionSpec as P

INTERPRET = False
F32 = jnp.float32
BF16 = jnp.bfloat16
VMEM = pl.BlockSpec(memory_space=pltpu.VMEM)
SMEM = pl.BlockSpec(memory_space=pltpu.SMEM)

CX, NY, CZ, KNOTS, SHARE = 4, 512, 128, 16, 64
GROUP = CZ // CX
CHUNK = 64


def iota(shape, dim):
    return lax.broadcasted_iota(jnp.int32, shape, dim)


def faces_kernel(vol_ref, out_ref):
    lane = iota((8, CZ), 1)
    for x in range(CX):
        packed = jnp.zeros((8, CZ), F32)
        for j in range(NY // 8):
            row = vol_ref[x, 8 * j : 8 * j + 8, :]
            moved = pltpu.roll(row, 2 * j, 1) if j else row
            keep = (lane == 2 * j) | (lane == (2 * j - 1) % CZ)
            packed = jnp.where(keep, moved, packed)
        out_ref[x] = packed


def pack_faces(volume):
    return pl.pallas_call(
        faces_kernel,
        out_shape=jax.ShapeDtypeStruct((CX, 8, CZ), F32),
        in_specs=[VMEM],
        out_specs=VMEM,
        name="faces",
        interpret=INTERPRET,
    )(volume)


def render_kernel(
    cells,
    vol_ref, low_ref, high_ref, near_ref, far_ref, resample_ref, transfer_ref, light_ref, bounds_ref,
    lower_ref, upper_ref,
    fields, samples, colors, parts, sums, masks, square, total,
):
    lane8 = iota((8, CZ), 1)
    square[...] = jnp.zeros_like(square)
    square[0:KNOTS, 0:4] = transfer_ref[...]
    knots = square[...].T[0:8]
    step = jnp.where(lane8 < KNOTS - 1, pltpu.roll(knots, CZ - 1, 1) - knots, 0.0)
    scale = jnp.where(iota((8, CZ), 0) == 3, -(2.0 / 1024) * math.log2(math.e), 1.0)
    slopes = step * scale
    bases = (knots - lane8.astype(F32) * step) * scale

    def table(rows, channel):
        return jnp.broadcast_to(rows[channel : channel + 1], (CHUNK, CZ))

    square[...] = jnp.zeros_like(square)
    limits = jnp.concatenate(
        [bounds_ref[...], jnp.ones((1, NY), F32), jnp.zeros((CZ - 17, NY), F32)], axis=0
    )
    limits = limits.T.astype(BF16)
    rows_i = iota((CZ, CZ), 0)
    cols_i = iota((CZ, CZ), 1)
    half = cols_i.astype(F32) + 0.5
    src = iota((2 * CZ, 2 * CZ), 0) % CZ
    dst_lane = iota((2 * CZ, 2 * CZ), 1)
    dst = dst_lane % CZ
    same = (src // GROUP) == (dst // GROUP)
    before = (src < dst) | ((src == dst) & (dst_lane >= CZ))
    prefix = jnp.where(same & before, 1.0, 0.0).astype(BF16)

    light0 = light_ref[0] * 0.7
    light1 = light_ref[1] * 0.7
    light2 = light_ref[2] * 0.7
    lane = iota((CHUNK, CZ), 1)

    for x in cells:
        packed = jnp.where(
            lane8 % 2 == 0, pltpu.roll(near_ref[x], 1, 1), pltpu.roll(far_ref[x], CZ - 1, 1)
        )
        for chunk in range(NY // CHUNK):
            r0 = chunk * CHUNK
            here = pl.ds(r0, CHUNK)
            f = vol_ref[x, here, :]
            below = low_ref[here, :] if x == 0 else vol_ref[x - 1, here, :]
            above = high_ref[here, :] if x == CX - 1 else vol_ref[x + 1, here, :]
            blank = jnp.zeros((1, CZ), F32)
            if r0 == 0:
                prev = jnp.concatenate([blank, vol_ref[x, 0 : CHUNK - 1, :]], axis=0)
            else:
                prev = vol_ref[x, r0 - 1 : r0 + CHUNK - 1, :]
            if r0 + CHUNK == NY:
                following = jnp.concatenate([vol_ref[x, r0 + 1 : NY, :], blank], axis=0)
            else:
                following = vol_ref[x, r0 + 1 : r0 + CHUNK + 1, :]
            ends = jnp.concatenate(
                [
                    pltpu.roll(packed, (CZ - 2 * j) % CZ, 1) if j else packed
                    for j in range(r0 // 8, (r0 + CHUNK) // 8)
                ],
                axis=0,
            )
            front = jnp.where(lane == 0, ends, pltpu.roll(f, 1, 1))
            back = jnp.where(lane == CZ - 1, ends, pltpu.roll(f, CZ - 1, 1))
            fields[here, 0:CZ] = f.astype(BF16)
            fields[here, CZ : 2 * CZ] = (above - below).astype(BF16)
            fields[here, 2 * CZ : 3 * CZ] = (following - prev).astype(BF16)
            fields[here, 3 * CZ : 4 * CZ] = (back - front).astype(BF16)
        for first, last, k0 in ((0, 192, 0), (192, 320, 128), (320, 512, 256)):
            samples[first:last, :] = jnp.dot(
                resample_ref[first:last, k0 : k0 + 256],
                fields[k0 : k0 + 256, :],
                preferred_element_type=F32,
            )
        pixel = x + cols_i // GROUP
        select = jnp.concatenate(
            [
                jnp.where(rows_i == pixel, -1.0, jnp.where(rows_i == 16, half, 0.0)),
                jnp.where(rows_i == pixel + 8, 1.0, jnp.where(rows_i == 16, -half, 0.0)),
            ],
            axis=1,
        ).astype(BF16)
        masks[...] = jnp.dot(limits, select, preferred_element_type=F32)

        def classify(chunk, carry):
            here = pl.ds(pl.multiple_of(chunk * CHUNK, CHUNK), CHUNK)
            d = samples[here, 0:CZ]
            gx = samples[here, CZ : 2 * CZ]
            gy = samples[here, 2 * CZ : 3 * CZ]
            gz = samples[here, 3 * CZ : 4 * CZ]
            t = jnp.clip(d * 3.0 + 7.5, 0.0, KNOTS - 1.0)
            knot = t.astype(jnp.int32)

            def lookup(channel):
                base = jnp.take_along_axis(
                    table(bases, channel), knot, axis=1, mode="promise_in_bounds"
                )
                slope = jnp.take_along_axis(
                    table(slopes, channel), knot, axis=1, mode="promise_in_bounds"
                )
                return base + t * slope

            lit = jnp.abs(gx * light0 + gy * light1 + gz * light2)
            lit = 0.3 + lit * lax.rsqrt(gx * gx + gy * gy + gz * gz + 4.0)
            inside = jnp.minimum(masks[here, 0:CZ], masks[here, CZ : 2 * CZ]) > 0.0
            tau = jnp.where(inside, lookup(3), 0.0)
            high = tau.astype(BF16)
            parts[here, 6 * CZ : 7 * CZ] = high
            parts[here, 7 * CZ : 8 * CZ] = (tau - high.astype(F32)).astype(BF16)
            for channel in range(3):
                colors[here, channel * CZ : (channel + 1) * CZ] = lookup(channel) * lit
            return carry

        lax.fori_loop(0, NY // CHUNK, classify, 0)
        sums[...] = jnp.dot(parts[:, 6 * CZ :], prefix, preferred_element_type=F32)

        def weigh(chunk, carry):
            here = pl.ds(pl.multiple_of(chunk * CHUNK, CHUNK), CHUNK)
            weight = jnp.exp2(sums[here, 0:CZ]) - jnp.exp2(sums[here, CZ : 2 * CZ])
            for channel in range(3):
                value = weight * colors[here, channel * CZ : (channel + 1) * CZ]
                high = value.astype(BF16)
                parts[here, 2 * channel * CZ : (2 * channel + 1) * CZ] = high
                parts[here, (2 * channel + 1) * CZ : (2 * channel + 2) * CZ] = (
                    value - high.astype(F32)
                ).astype(BF16)
            return carry

        lax.fori_loop(0, NY // CHUNK, weigh, 0)
        row = iota((8 * CZ, CZ), 0)
        group = (row % CZ) // GROUP
        place = (group * 4 + row // (2 * CZ)) * 8 + x + group
        gather = jnp.where(iota((8 * CZ, CZ), 1) == place, 1.0, 0.0).astype(BF16)
        part = jnp.dot(parts[...], gather, preferred_element_type=F32)
        if x == cells[0]:
            total[...] = part
        else:
            total[...] += part

    image = total[...].T
    depth = jnp.zeros((8, NY), F32)
    color = [jnp.zeros((8, NY), F32) for _ in range(3)]
    for group in range(CX):
        through = jnp.exp2(depth)
        for channel in range(3):
            at = (group * 4 + channel) * 8
            color[channel] = color[channel] + through * image[at : at + 8]
        at = (group * 4 + 3) * 8
        depth = depth + image[at : at + 8]
    planes = color + [depth]
    sub = iota((8, CZ), 0)
    lane = iota((8, CZ), 1)
    for m in range(NY // CZ):
        tile = [plane[:, m * CZ : (m + 1) * CZ] for plane in planes]
        turned = [pltpu.roll(part, 4, 0) for part in tile]
        for ref, a, b in (
            (lower_ref, jnp.where(sub < 4, tile[0], turned[1]), jnp.where(sub < 4, tile[2], turned[3])),
            (upper_ref, jnp.where(sub < 4, turned[0], tile[1]), jnp.where(sub < 4, turned[2], tile[3])),
        ):
            ref[2 * m] = jnp.where(lane < SHARE, a, pltpu.roll(b, SHARE, 1))
            ref[2 * m + 1] = jnp.where(lane < SHARE, pltpu.roll(a, SHARE, 1), b)


def render(volume, low, high, near, far, resample, transfer, light, bounds):
    block = jax.ShapeDtypeStruct((8, 8, CZ), F32)
    return pl.pallas_call(
        functools.partial(render_kernel, tuple(range(CX))),
        out_shape=(block, block),
        in_specs=[VMEM] * 7 + [SMEM] + [VMEM],
        out_specs=(VMEM, VMEM),
        scratch_shapes=[
            pltpu.VMEM((NY, 4 * CZ), BF16),
            pltpu.VMEM((NY, 4 * CZ), F32),
            pltpu.VMEM((NY, 3 * CZ), F32),
            pltpu.VMEM((NY, 8 * CZ), BF16),
            pltpu.VMEM((NY, 2 * CZ), F32),
            pltpu.VMEM((NY, 2 * CZ), F32),
            pltpu.VMEM((CZ, CZ), F32),
            pltpu.VMEM((NY, CZ), F32),
        ],
        name="render",
        interpret=INTERPRET,
    )(volume, low, high, near, far, resample, transfer, light, bounds)


def fold_kernel(pieces_ref, out_ref):
    sub = iota((8, CZ), 0)
    lane = iota((8, CZ), 1)
    color = jnp.zeros((8, CZ), F32)
    depth = jnp.zeros((8, CZ), F32)
    for d in range(pieces_ref.shape[0]):
        for side in range(2):
            piece = pieces_ref[d, side]
            own = jnp.where(lane >= SHARE, piece, pltpu.roll(piece, SHARE, 1))
            own = jnp.where(sub >= 4, own, pltpu.roll(own, 4, 0))
            color = color + jnp.exp2(depth) * piece
            depth = depth + own
    opacity = 1.0 - jnp.exp2(depth)
    color = jnp.where((sub >= 4) & (lane >= SHARE), opacity, color)
    turned = pltpu.roll(color, SHARE, 1)
    out_ref[0] = color[0:4, 0:SHARE]
    out_ref[1] = color[4:8, 0:SHARE]
    out_ref[2] = turned[0:4, 0:SHARE]
    out_ref[3] = turned[4:8, 0:SHARE]


def fold(pieces):
    return pl.pallas_call(
        fold_kernel,
        out_shape=jax.ShapeDtypeStruct((4, CX, SHARE), F32),
        in_specs=[VMEM],
        out_specs=VMEM,
        name="fold",
        interpret=INTERPRET,
    )(pieces)


def body(volume, resample, transfer, light, ray_bounds):
    planes = lax.axis_size("plane")
    depths = lax.axis_size("depth")
    plane_index = lax.axis_index("plane")
    depth_index = lax.axis_index("depth")

    def shifted(value, axis, steps):
        count = lax.axis_size(axis)
        pairs = [(i, i + steps) for i in range(count) if 0 <= i + steps < count]
        return lax.ppermute(value, axis, pairs)

    low = shifted(volume[CX - 1], "plane", 1)
    high = shifted(volume[0], "plane", -1)
    faces = pack_faces(volume)
    near = shifted(faces, "depth", 1)
    far = shifted(faces, "depth", -1)

    def bound_rows(block):
        start = jnp.minimum(block, planes - 1) * CX
        return lax.dynamic_slice_in_dim(ray_bounds, start, CX, 1)

    column_block = plane_index + depth_index
    bounds = jnp.concatenate([bound_rows(column_block), bound_rows(column_block + 1)], axis=1)
    bounds = jnp.clip(bounds - depth_index * CZ, 0, CZ).astype(F32).reshape(2 * 8, NY)

    lower, upper = render(volume, low, high, near, far, resample, transfer, light, bounds)

    def skewed(value, extra):
        pairs = [
            (p * depths + d, (p + d + extra) * depths + d)
            for p in range(planes)
            for d in range(depths)
            if p + d + extra < planes
        ]
        return lax.ppermute(value, ("plane", "depth"), pairs)

    pieces = jnp.stack([skewed(lower, 0), skewed(upper, 1)], axis=1)
    pieces = lax.all_to_all(pieces, "depth", 0, 0, tiled=True)
    return fold(pieces)


def solution(mesh):
    in_specs = (P("plane", None, "depth"), P(), P(), P(), P())
    out_specs = P(None, "plane", "depth")
    return jax.shard_map(body, mesh=mesh, in_specs=in_specs, out_specs=out_specs, check_vma=False)
```

```python
import functools
import math

import jax
import jax.numpy as jnp
import numpy as np
from jax import lax
from jax.experimental import pallas as pl
from jax.experimental.pallas import tpu as pltpu
from jax.sharding import PartitionSpec as P

INTERPRET = False
F32 = jnp.float32
BF16 = jnp.bfloat16
VMEM = pl.BlockSpec(memory_space=pltpu.VMEM)
SMEM = pl.BlockSpec(memory_space=pltpu.SMEM)

CX, NY, CZ, KNOTS, SHARE = 4, 512, 128, 16, 64
GROUP = CZ // CX
CHUNK = 64
WROWS = 16
LIMIT = 36 << 20


def matmul(a, b):
    return jnp.dot(a, b, preferred_element_type=F32)


def iota(shape, dim):
    return lax.broadcasted_iota(jnp.int32, shape, dim)


def prepare_kernel(vol_ref, transfer_ref, bounds_ref, out_ref, tables_ref, limits_ref, window, square, sem):
    planes = bounds_ref.shape[1] // CX
    column = CX * (lax.axis_index("plane") + lax.axis_index("depth"))
    start = pl.multiple_of(jnp.minimum((column // 8) * 8, planes * CX - 16), 8)
    copy = pltpu.make_async_copy(bounds_ref.at[:, pl.ds(start, 16), :], window, sem)
    copy.start()
    lane = iota((8, CZ), 1)
    for x in range(CX):
        packed = jnp.zeros((8, CZ), F32)
        for j in range(NY // 8):
            row = vol_ref[x, 8 * j : 8 * j + 8, :]
            moved = pltpu.roll(row, 2 * j, 1) if j else row
            keep = (lane == 2 * j) | (lane == (2 * j - 1) % CZ)
            packed = jnp.where(keep, moved, packed)
        out_ref[x] = packed
    square[...] = jnp.zeros_like(square)
    square[0:4, 0:KNOTS] = transfer_ref[...]
    knots = square[...]
    step = jnp.where(lane < KNOTS - 1, pltpu.roll(knots, CZ - 1, 1) - knots, 0.0)
    scale = jnp.where(iota((8, CZ), 0) == 3, -(2.0 / 1024) * math.log2(math.e), 1.0)
    tables_ref[0] = (knots - lane.astype(F32) * step) * scale
    tables_ref[1] = step * scale
    copy.wait()
    base = lax.axis_index("depth") * CZ
    turn = 16 - jnp.minimum(column - start, 15)
    ends = jnp.clip(window[...] - base, 0, CZ).astype(F32)
    first = pltpu.roll(ends[0], turn, 0)[0:8]
    last = pltpu.roll(ends[1], turn, 0)[0:8]
    limits = jnp.concatenate(
        [first, last, jnp.ones((1, NY), F32), jnp.zeros((CZ - 17, NY), F32)], axis=0
    )
    limits_ref[...] = limits.T.astype(BF16)


def prepare(volume, transfer, ray_bounds):
    return pl.pallas_call(
        prepare_kernel,
        out_shape=(
            jax.ShapeDtypeStruct((CX, 8, CZ), F32),
            jax.ShapeDtypeStruct((2, 8, CZ), F32),
            jax.ShapeDtypeStruct((NY, CZ), BF16),
        ),
        in_specs=[VMEM, VMEM, pl.BlockSpec(memory_space=pl.ANY)],
        out_specs=(VMEM, VMEM, VMEM),
        scratch_shapes=[
            pltpu.VMEM((2, 16, NY), jnp.int32),
            pltpu.VMEM((8, CZ), F32),
            pltpu.SemaphoreType.DMA,
        ],
        compiler_params=pltpu.CompilerParams(vmem_limit_bytes=LIMIT),
        name="prepare",
        interpret=INTERPRET,
    )(volume, transfer.T, ray_bounds)


def constants():
    src = np.arange(2 * CZ)[:, None] % CZ
    lane = np.arange(2 * CZ)[None, :]
    dst = lane % CZ
    before = (src < dst) | ((src == dst) & (lane >= CZ))
    prefix = (src // GROUP == dst // GROUP) & before
    row = np.arange(CZ)[None, :, None]
    z = np.arange(CZ)[None, None, :]
    pixel = np.arange(CX)[:, None, None] + z // GROUP
    ahead = np.where(row == pixel, -1.0, np.where(row == 16, z + 0.5, 0.0))
    behind = np.where(row == pixel + 8, 1.0, np.where(row == 16, -(z + 0.5), 0.0))
    select = np.concatenate([ahead, behind], axis=2)
    row = np.arange(8 * CZ)[None, :, None]
    group = (row % CZ) // GROUP
    place = (group * 4 + row // (2 * CZ)) * 8 + np.arange(CX)[:, None, None] + group
    gather = np.arange(CZ)[None, None, :] == place
    return [jnp.asarray(np.asarray(a, np.float32), BF16) for a in (prefix, select, gather)]


def render_kernel(
    cells,
    vol_ref, low_ref, high_ref, near_ref, far_ref, resample_ref, tables_ref, light_ref, limits_ref,
    prefix_ref, select_ref, gather_ref,
    lower_ref, upper_ref,
    total, *buffers,
):
    lane8 = iota((8, CZ), 1)
    tables = [
        [jnp.broadcast_to(tables_ref[i, c : c + 1], (8, CZ)) for c in range(4)] for i in range(2)
    ]
    light0 = light_ref[0] * 0.7
    light1 = light_ref[1] * 0.7
    light2 = light_ref[2] * 0.7
    lane = iota((CHUNK, CZ), 1)

    for x in cells:
        fields, samples, colors, parts, sums, masks, taus = (buffer.at[x] for buffer in buffers)
        packed = jnp.where(
            lane8 % 2 == 0, pltpu.roll(near_ref[x], 1, 1), pltpu.roll(far_ref[x], CZ - 1, 1)
        )
        for chunk in range(NY // CHUNK):
            r0 = chunk * CHUNK
            here = pl.ds(r0, CHUNK)
            f = vol_ref[x, here, :]
            below = low_ref[here, :] if x == 0 else vol_ref[x - 1, here, :]
            above = high_ref[here, :] if x == CX - 1 else vol_ref[x + 1, here, :]
            blank = jnp.zeros((1, CZ), F32)
            if r0 == 0:
                prev = jnp.concatenate([blank, vol_ref[x, 0 : CHUNK - 1, :]], axis=0)
            else:
                prev = vol_ref[x, r0 - 1 : r0 + CHUNK - 1, :]
            if r0 + CHUNK == NY:
                following = jnp.concatenate([vol_ref[x, r0 + 1 : NY, :], blank], axis=0)
            else:
                following = vol_ref[x, r0 + 1 : r0 + CHUNK + 1, :]
            ends = jnp.concatenate(
                [
                    pltpu.roll(packed, (CZ - 2 * j) % CZ, 1) if j else packed
                    for j in range(r0 // 8, (r0 + CHUNK) // 8)
                ],
                axis=0,
            )
            front = jnp.where(lane == 0, ends, pltpu.roll(f, 1, 1))
            back = jnp.where(lane == CZ - 1, ends, pltpu.roll(f, CZ - 1, 1))
            fields[here, 0:CZ] = f.astype(BF16)
            fields[here, CZ : 2 * CZ] = (above - below).astype(BF16)
            fields[here, 2 * CZ : 3 * CZ] = (following - prev).astype(BF16)
            fields[here, 3 * CZ : 4 * CZ] = (back - front).astype(BF16)
        for first, last, k0 in ((0, 192, 0), (192, 320, 128), (320, 512, 256)):
            samples[first:last, :] = matmul(
                resample_ref[first:last, k0 : k0 + 256], fields[k0 : k0 + 256, :]
            )
        masks[...] = matmul(limits_ref[...], select_ref[x])

        if True:
            for row in range(0, NY, 8):
                here = pl.ds(row, 8)
                d = samples[here, 0:CZ]
                gx = samples[here, CZ : 2 * CZ]
                gy = samples[here, 2 * CZ : 3 * CZ]
                gz = samples[here, 3 * CZ : 4 * CZ]
                t = jnp.clip(d * 3.0 + 7.5, 0.0, KNOTS - 1.0)
                knot = t.astype(jnp.int32)

                def lookup(channel):
                    base = jnp.take_along_axis(
                        tables[0][channel], knot, axis=1, mode="promise_in_bounds"
                    )
                    slope = jnp.take_along_axis(
                        tables[1][channel], knot, axis=1, mode="promise_in_bounds"
                    )
                    return base + t * slope

                lit = jnp.abs(gx * light0 + gy * light1 + gz * light2)
                lit = 0.3 + lit * lax.rsqrt(gx * gx + gy * gy + gz * gz + 4.0)
                inside = jnp.minimum(masks[here, 0:CZ], masks[here, CZ : 2 * CZ]) > 0.0
                tau = jnp.where(inside, lookup(3), 0.0)
                taus[here, :] = tau
                for channel in range(3):
                    colors[here, channel * CZ : (channel + 1) * CZ] = lookup(channel) * lit
        high = taus[...].astype(BF16)
        parts[:, 6 * CZ : 7 * CZ] = high
        parts[:, 7 * CZ :] = (taus[...] - high.astype(F32)).astype(BF16)
        sums[...] = matmul(parts[:, 6 * CZ :], prefix_ref[...])

        for row in range(0, NY, WROWS):
            here = pl.ds(row, WROWS)
            weight = jnp.exp2(sums[here, 0:CZ]) - jnp.exp2(sums[here, CZ : 2 * CZ])
            for channel in range(3):
                value = weight * colors[here, channel * CZ : (channel + 1) * CZ]
                high = value.astype(BF16)
                parts[here, 2 * channel * CZ : (2 * channel + 1) * CZ] = high
                parts[here, (2 * channel + 1) * CZ : (2 * channel + 2) * CZ] = (
                    value - high.astype(F32)
                ).astype(BF16)
        part = matmul(parts[...], gather_ref[x])
        if x == cells[0]:
            total[...] = part
        else:
            total[...] += part

    image = total[...].T
    depth = jnp.zeros((8, NY), F32)
    color = [jnp.zeros((8, NY), F32) for _ in range(3)]
    for group in range(CX):
        through = jnp.exp2(depth)
        for channel in range(3):
            at = (group * 4 + channel) * 8
            color[channel] = color[channel] + through * image[at : at + 8]
        at = (group * 4 + 3) * 8
        depth = depth + image[at : at + 8]
    planes = color + [depth]
    sub = iota((8, CZ), 0)
    lane = iota((8, CZ), 1)
    for m in range(NY // CZ):
        tile = [plane[:, m * CZ : (m + 1) * CZ] for plane in planes]
        turned = [pltpu.roll(part, 4, 0) for part in tile]
        for ref, a, b in (
            (lower_ref, jnp.where(sub < 4, tile[0], turned[1]), jnp.where(sub < 4, tile[2], turned[3])),
            (upper_ref, jnp.where(sub < 4, turned[0], tile[1]), jnp.where(sub < 4, turned[2], tile[3])),
        ):
            ref[2 * m] = jnp.where(lane < SHARE, a, pltpu.roll(b, SHARE, 1))
            ref[2 * m + 1] = jnp.where(lane < SHARE, pltpu.roll(a, SHARE, 1), b)


def render(*operands):
    block = jax.ShapeDtypeStruct((8, 8, CZ), F32)
    return pl.pallas_call(
        functools.partial(render_kernel, tuple(range(CX))),
        out_shape=(block, block),
        in_specs=[VMEM] * 7 + [SMEM] + [VMEM] * 4,
        out_specs=(VMEM, VMEM),
        scratch_shapes=[pltpu.VMEM((NY, CZ), F32)]
        + [
            pltpu.VMEM((CX, NY, width * CZ), kind)
            for width, kind in ((4, BF16), (4, F32), (3, F32), (8, BF16), (2, F32), (2, F32), (1, F32))
        ],
        compiler_params=pltpu.CompilerParams(vmem_limit_bytes=LIMIT),
        name="render",
        interpret=INTERPRET,
    )(*operands)


def fold_kernel(pieces_ref, out_ref):
    sub = iota((8, CZ), 0)
    lane = iota((8, CZ), 1)
    color = jnp.zeros((8, CZ), F32)
    depth = jnp.zeros((8, CZ), F32)
    for d in range(pieces_ref.shape[0]):
        for side in range(2):
            piece = pieces_ref[d, side]
            own = jnp.where(lane >= SHARE, piece, pltpu.roll(piece, SHARE, 1))
            own = jnp.where(sub >= 4, own, pltpu.roll(own, 4, 0))
            color = color + jnp.exp2(depth) * piece
            depth = depth + own
    opacity = 1.0 - jnp.exp2(depth)
    color = jnp.where((sub >= 4) & (lane >= SHARE), opacity, color)
    turned = pltpu.roll(color, SHARE, 1)
    out_ref[0] = color[0:4, 0:SHARE]
    out_ref[1] = color[4:8, 0:SHARE]
    out_ref[2] = turned[0:4, 0:SHARE]
    out_ref[3] = turned[4:8, 0:SHARE]


def fold(pieces):
    return pl.pallas_call(
        fold_kernel,
        out_shape=jax.ShapeDtypeStruct((4, CX, SHARE), F32),
        in_specs=[VMEM],
        out_specs=VMEM,
        compiler_params=pltpu.CompilerParams(vmem_limit_bytes=LIMIT),
        name="fold",
        interpret=INTERPRET,
    )(pieces)


def body(volume, resample, transfer, light, ray_bounds):
    planes = lax.axis_size("plane")
    depths = lax.axis_size("depth")

    def shifted(value, axis, steps):
        count = lax.axis_size(axis)
        pairs = [(i, i + steps) for i in range(count) if 0 <= i + steps < count]
        return lax.ppermute(value, axis, pairs)

    low = shifted(volume[CX - 1], "plane", 1)
    high = shifted(volume[0], "plane", -1)
    faces, tables, limits = prepare(volume, transfer, ray_bounds)
    near = shifted(faces, "depth", 1)
    far = shifted(faces, "depth", -1)
    lower, upper = render(
        volume, low, high, near, far, resample, tables, light, limits, *constants()
    )

    def skewed(value, extra):
        pairs = [
            (p * depths + d, (p + d + extra) * depths + d)
            for p in range(planes)
            for d in range(depths)
            if p + d + extra < planes
        ]
        return lax.ppermute(value, ("plane", "depth"), pairs)

    pieces = jnp.stack([skewed(lower, 0), skewed(upper, 1)], axis=1)
    pieces = lax.all_to_all(pieces, "depth", 0, 0, tiled=True)
    return fold(pieces)


def solution(mesh):
    in_specs = (P("plane", None, "depth"), P(), P(), P(), P())
    out_specs = P(None, "plane", "depth")
    return jax.shard_map(body, mesh=mesh, in_specs=in_specs, out_specs=out_specs, check_vma=False)
```

```python
import functools
import math

import jax
import jax.numpy as jnp
import numpy as np
from jax import lax
from jax.experimental import pallas as pl
from jax.experimental.pallas import tpu as pltpu
from jax.sharding import PartitionSpec as P

INTERPRET = False
F32 = jnp.float32
BF16 = jnp.bfloat16
VMEM = pl.BlockSpec(memory_space=pltpu.VMEM)
SMEM = pl.BlockSpec(memory_space=pltpu.SMEM)

CX, NY, CZ, KNOTS, SHARE = 4, 512, 128, 16, 64
GROUP = CZ // CX
CHUNK = 64
WROWS = 16
HALF = 256
LIMIT = 36 << 20


def matmul(a, b):
    return jnp.dot(a, b, preferred_element_type=F32)


def along(table, index):
    numbers = lax.GatherDimensionNumbers(
        offset_dims=(),
        collapsed_slice_dims=(1,),
        start_index_map=(1,),
        operand_batching_dims=(0,),
        start_indices_batching_dims=(0,),
    )
    mode = lax.GatherScatterMode.PROMISE_IN_BOUNDS
    return lax.gather(table, index[..., None], numbers, slice_sizes=(1, 1), mode=mode)


def iota(shape, dim):
    return lax.broadcasted_iota(jnp.int32, shape, dim)


def prepare_kernel(
    vol_ref, transfer_ref, light_ref, bounds_ref, out_ref, tables_ref, limits_ref, window, square, sem
):
    planes = bounds_ref.shape[1] // CX
    column = CX * (lax.axis_index("plane") + lax.axis_index("depth"))
    start = pl.multiple_of(jnp.minimum((column // 8) * 8, planes * CX - 16), 8)
    copy = pltpu.make_async_copy(bounds_ref.at[:, pl.ds(start, 16), :], window, sem)
    copy.start()
    lane = iota((8, CZ), 1)
    for x in range(CX):
        packed = jnp.zeros((8, CZ), F32)
        for j in range(NY // 8):
            row = vol_ref[x, 8 * j : 8 * j + 8, :]
            moved = pltpu.roll(row, 2 * j, 1) if j else row
            keep = (lane == 2 * j) | (lane == (2 * j - 1) % CZ)
            packed = jnp.where(keep, moved, packed)
        out_ref[x] = packed
    square[...] = jnp.zeros_like(square)
    square[0:4, 0:KNOTS] = transfer_ref[...]
    knots = square[...]
    step = jnp.where(lane < KNOTS - 1, pltpu.roll(knots, CZ - 1, 1) - knots, 0.0)
    scale = jnp.where(iota((8, CZ), 0) == 3, -(2.0 / 1024) * math.log2(math.e), 1.0)
    tables_ref[0] = (knots - lane.astype(F32) * step) * scale
    tables_ref[1] = step * scale
    tables_ref[2] = jnp.zeros((8, CZ), F32)
    for axis in range(3):
        tables_ref[2, axis : axis + 1] = jnp.broadcast_to(light_ref[axis] * 0.7, (1, CZ))
    copy.wait()
    base = lax.axis_index("depth") * CZ
    turn = 16 - jnp.minimum(column - start, 15)
    ends = jnp.clip(window[...] - base, 0, CZ).astype(F32)
    first = pltpu.roll(ends[0], turn, 0)[0:8]
    last = pltpu.roll(ends[1], turn, 0)[0:8]
    limits = jnp.concatenate(
        [first, last, jnp.ones((1, NY), F32), jnp.zeros((CZ - 17, NY), F32)], axis=0
    )
    limits_ref[...] = limits.T.astype(BF16)


def prepare(volume, transfer, light, ray_bounds):
    return pl.pallas_call(
        prepare_kernel,
        out_shape=(
            jax.ShapeDtypeStruct((CX, 8, CZ), F32),
            jax.ShapeDtypeStruct((3, 8, CZ), F32),
            jax.ShapeDtypeStruct((NY, CZ), BF16),
        ),
        in_specs=[VMEM, VMEM, SMEM, pl.BlockSpec(memory_space=pltpu.HBM)],
        out_specs=(VMEM, VMEM, VMEM),
        scratch_shapes=[
            pltpu.VMEM((2, 16, NY), jnp.int32),
            pltpu.VMEM((8, CZ), F32),
            pltpu.SemaphoreType.DMA,
        ],
        compiler_params=pltpu.CompilerParams(vmem_limit_bytes=LIMIT),
        name="prepare",
        interpret=INTERPRET,
    )(volume, transfer.T, light, ray_bounds)


def constants():
    src = np.arange(2 * CZ)[:, None] % CZ
    lane = np.arange(2 * CZ)[None, :]
    dst = lane % CZ
    before = (src < dst) | ((src == dst) & (lane >= CZ))
    prefix = (src // GROUP == dst // GROUP) & before
    row = np.arange(CZ)[None, :, None]
    z = np.arange(CZ)[None, None, :]
    pixel = np.arange(CX)[:, None, None] + z // GROUP
    ahead = np.where(row == pixel, -1.0, np.where(row == 16, z + 0.5, 0.0))
    behind = np.where(row == pixel + 8, 1.0, np.where(row == 16, -(z + 0.5), 0.0))
    select = np.concatenate([ahead, behind], axis=2)
    row = np.arange(8 * CZ)[None, :, None]
    group = (row % CZ) // GROUP
    place = (group * 4 + row // (2 * CZ)) * 8 + np.arange(CX)[:, None, None] + group
    gather = np.arange(CZ)[None, None, :] == place
    return [jnp.asarray(np.asarray(a, np.float32), BF16) for a in (prefix, select, gather)]


def render_kernel(
    cells,
    vol_ref, plane_even_ref, plane_odd_ref, depth_even_ref, depth_odd_ref,
    resample_ref, tables_ref, limits_ref,
    prefix_ref, select_ref, gather_ref,
    lower_ref, upper_ref,
    total, *buffers,
):
    lane8 = iota((8, CZ), 1)
    tables = [
        [jnp.broadcast_to(tables_ref[i, c : c + 1], (8, CZ)) for c in range(4)] for i in range(2)
    ]
    light0, light1, light2 = (
        jnp.broadcast_to(tables_ref[2, c : c + 1], (8, CZ)) for c in range(3)
    )
    plane_odd = lax.axis_index("plane") % 2 == 1
    depth_odd = lax.axis_index("depth") % 2 == 1
    lane = iota((CHUNK, CZ), 1)
    each = [[buffer.at[x] for buffer in buffers] for x in range(CX)]
    packed = {
        x: jnp.where(
            lane8 % 2 == 0,
            pltpu.roll(jnp.where(depth_odd, depth_even_ref[x], depth_odd_ref[x]), 1, 1),
            pltpu.roll(jnp.where(depth_odd, depth_odd_ref[x], depth_even_ref[x]), CZ - 1, 1),
        )
        for x in cells
    }

    def beside(x, here):
        if x < 0:
            return jnp.where(plane_odd, plane_even_ref[here, :], plane_odd_ref[here, :])
        if x == CX:
            return jnp.where(plane_odd, plane_odd_ref[here, :], plane_even_ref[here, :])
        return vol_ref[x, here, :]

    def differences(x, chunk):
        fields = each[x][0]
        r0 = chunk * CHUNK
        here = pl.ds(r0, CHUNK)
        f = vol_ref[x, here, :]
        below = beside(x - 1, here)
        above = beside(x + 1, here)
        blank = jnp.zeros((1, CZ), F32)
        if r0 == 0:
            prev = jnp.concatenate([blank, vol_ref[x, 0 : CHUNK - 1, :]], axis=0)
        else:
            prev = vol_ref[x, r0 - 1 : r0 + CHUNK - 1, :]
        if r0 + CHUNK == NY:
            following = jnp.concatenate([vol_ref[x, r0 + 1 : NY, :], blank], axis=0)
        else:
            following = vol_ref[x, r0 + 1 : r0 + CHUNK + 1, :]
        ends = jnp.concatenate(
            [
                pltpu.roll(packed[x], (CZ - 2 * j) % CZ, 1) if j else packed[x]
                for j in range(r0 // 8, (r0 + CHUNK) // 8)
            ],
            axis=0,
        )
        front = jnp.where(lane == 0, ends, pltpu.roll(f, 1, 1))
        back = jnp.where(lane == CZ - 1, ends, pltpu.roll(f, CZ - 1, 1))
        fields[here, 0:CZ] = f.astype(BF16)
        fields[here, CZ : 2 * CZ] = (above - below).astype(BF16)
        fields[here, 2 * CZ : 3 * CZ] = (following - prev).astype(BF16)
        fields[here, 3 * CZ : 4 * CZ] = (back - front).astype(BF16)

    def resampled(x, window):
        fields, samples = each[x][:2]
        first, last, k0 = ((0, 192, 0), (192, 320, 128), (320, 512, 256))[window]
        samples[first:last, :] = matmul(
            resample_ref[first:last, k0 : k0 + 256], fields[k0 : k0 + 256, :]
        )

    def distances(x):
        each[x][5][...] = matmul(limits_ref[...], select_ref[x])

    def classify(x, chunk):
        _, samples, colors, parts, _, masks = each[x]
        for row in range(chunk * CHUNK, (chunk + 1) * CHUNK, 8):
            here = pl.ds(row, 8)
            d = samples[here, 0:CZ]
            gx = samples[here, CZ : 2 * CZ]
            gy = samples[here, 2 * CZ : 3 * CZ]
            gz = samples[here, 3 * CZ : 4 * CZ]
            t = jnp.clip(d * 3.0 + 7.5, 0.0, KNOTS - 1.0)
            knot = t.astype(jnp.int32)

            def lookup(channel):
                return along(tables[0][channel], knot) + t * along(tables[1][channel], knot)

            lit = jnp.abs(gx * light0 + gy * light1 + gz * light2)
            lit = 0.3 + lit * lax.rsqrt(gx * gx + gy * gy + gz * gz + 4.0)
            inside = jnp.minimum(masks[here, 0:CZ], masks[here, CZ : 2 * CZ]) > 0.0
            tau = jnp.where(inside, lookup(3), 0.0)
            high = tau.astype(BF16)
            parts[here, 6 * CZ : 7 * CZ] = high
            parts[here, 7 * CZ : 8 * CZ] = (tau - high.astype(F32)).astype(BF16)
            for channel in range(3):
                colors[here, channel * CZ : (channel + 1) * CZ] = lookup(channel) * lit

    def depths(x, half):
        here = pl.ds(half * HALF, HALF)
        each[x][4][here, :] = matmul(each[x][3][here, 6 * CZ :], prefix_ref[...])

    def weigh(x, chunk):
        _, _, colors, parts, sums, _ = each[x]
        for row in range(chunk * CHUNK, (chunk + 1) * CHUNK, WROWS):
            here = pl.ds(row, WROWS)
            weight = jnp.exp2(sums[here, 0:CZ]) - jnp.exp2(sums[here, CZ : 2 * CZ])
            for channel in range(3):
                value = weight * colors[here, channel * CZ : (channel + 1) * CZ]
                high = value.astype(BF16)
                parts[here, 2 * channel * CZ : (2 * channel + 1) * CZ] = high
                parts[here, (2 * channel + 1) * CZ : (2 * channel + 2) * CZ] = (
                    value - high.astype(F32)
                ).astype(BF16)

    def gathered(x, half):
        here = pl.ds(half * HALF, HALF)
        part = matmul(each[x][3][here, :], gather_ref[x])
        if x == cells[0]:
            total[here, :] = part
        else:
            total[here, :] += part

    count = NY // CHUNK
    middle = count // 2
    for step in range(-1, len(cells) + 1):
        now = cells[step] if 0 <= step < len(cells) else None
        after = cells[step + 1] if step + 1 < len(cells) else None
        past = cells[step - 1] if step > 0 else None
        for chunk in range(count):
            if now is not None:
                classify(now, chunk)
            if after is not None:
                differences(after, chunk)
            if chunk >= middle and now is not None:
                weigh(now, chunk - middle)
            if chunk < middle and past is not None:
                weigh(past, chunk + middle)
            if chunk == middle - 1:
                if now is not None:
                    depths(now, 0)
                if past is not None:
                    gathered(past, 1)
                if after is not None:
                    resampled(after, 0)
            if chunk == middle + 1 and after is not None:
                resampled(after, 1)
        if now is not None:
            depths(now, 1)
            gathered(now, 0)
        if after is not None:
            resampled(after, 2)
            distances(after)

    image = total[...].T
    depth = jnp.zeros((8, NY), F32)
    color = [jnp.zeros((8, NY), F32) for _ in range(3)]
    for group in range(CX):
        through = jnp.exp2(depth)
        for channel in range(3):
            at = (group * 4 + channel) * 8
            color[channel] = color[channel] + through * image[at : at + 8]
        at = (group * 4 + 3) * 8
        depth = depth + image[at : at + 8]
    planes = color + [depth]
    sub = iota((8, CZ), 0)
    lane = iota((8, CZ), 1)
    for m in range(NY // CZ):
        tile = [plane[:, m * CZ : (m + 1) * CZ] for plane in planes]
        turned = [pltpu.roll(part, 4, 0) for part in tile]
        for ref, a, b in (
            (lower_ref, jnp.where(sub < 4, tile[0], turned[1]), jnp.where(sub < 4, tile[2], turned[3])),
            (upper_ref, jnp.where(sub < 4, turned[0], tile[1]), jnp.where(sub < 4, turned[2], tile[3])),
        ):
            ref[2 * m] = jnp.where(lane < SHARE, a, pltpu.roll(b, SHARE, 1))
            ref[2 * m + 1] = jnp.where(lane < SHARE, pltpu.roll(a, SHARE, 1), b)


def render(*operands):
    block = jax.ShapeDtypeStruct((8, 8, CZ), F32)
    return pl.pallas_call(
        functools.partial(render_kernel, tuple(range(CX))),
        out_shape=(block, block),
        in_specs=[VMEM] * 11,
        out_specs=(VMEM, VMEM),
        scratch_shapes=[pltpu.VMEM((NY, CZ), F32)]
        + [
            pltpu.VMEM((CX, NY, width * CZ), kind)
            for width, kind in ((4, BF16), (4, F32), (3, F32), (8, BF16), (2, F32), (2, F32))
        ],
        compiler_params=pltpu.CompilerParams(vmem_limit_bytes=LIMIT),
        name="render",
        interpret=INTERPRET,
    )(*operands)


def fold_kernel(pieces_ref, out_ref):
    sub = iota((8, CZ), 0)
    lane = iota((8, CZ), 1)
    color = jnp.zeros((8, CZ), F32)
    depth = jnp.zeros((8, CZ), F32)
    for d in range(pieces_ref.shape[0]):
        for side in range(2):
            piece = pieces_ref[d, side]
            own = jnp.where(lane >= SHARE, piece, pltpu.roll(piece, SHARE, 1))
            own = jnp.where(sub >= 4, own, pltpu.roll(own, 4, 0))
            color = color + jnp.exp2(depth) * piece
            depth = depth + own
    opacity = 1.0 - jnp.exp2(depth)
    color = jnp.where((sub >= 4) & (lane >= SHARE), opacity, color)
    turned = pltpu.roll(color, SHARE, 1)
    out_ref[0] = color[0:4, 0:SHARE]
    out_ref[1] = color[4:8, 0:SHARE]
    out_ref[2] = turned[0:4, 0:SHARE]
    out_ref[3] = turned[4:8, 0:SHARE]


def fold(pieces):
    return pl.pallas_call(
        fold_kernel,
        out_shape=jax.ShapeDtypeStruct((4, CX, SHARE), F32),
        in_specs=[VMEM],
        out_specs=VMEM,
        compiler_params=pltpu.CompilerParams(vmem_limit_bytes=LIMIT),
        name="fold",
        interpret=INTERPRET,
    )(pieces)


def body(volume, resample, transfer, light, ray_bounds):
    planes = lax.axis_size("plane")
    depths = lax.axis_size("depth")

    def exchanged(value, axis, first):
        pairs = []
        for i in range(first, lax.axis_size(axis) - 1, 2):
            pairs += [(i, i + 1), (i + 1, i)]
        return lax.ppermute(value, axis, pairs)

    odd = lax.axis_index("plane") % 2
    outward = lax.dynamic_index_in_dim(volume, (CX - 1) * (1 - odd), 0, keepdims=False)
    inward = lax.dynamic_index_in_dim(volume, (CX - 1) * odd, 0, keepdims=False)
    plane_even = exchanged(outward, "plane", 0)
    plane_odd = exchanged(inward, "plane", 1)
    faces, tables, limits = prepare(volume, transfer, light, ray_bounds)
    depth_even = exchanged(faces, "depth", 0)
    depth_odd = exchanged(faces, "depth", 1)
    lower, upper = render(
        volume, plane_even, plane_odd, depth_even, depth_odd,
        resample, tables, limits, *constants(),
    )

    def skewed(value, extra):
        pairs = [
            (p * depths + d, (p + d + extra) * depths + d)
            for p in range(planes)
            for d in range(depths)
            if p + d + extra < planes
        ]
        return lax.ppermute(value, ("plane", "depth"), pairs)

    pieces = jnp.stack([skewed(lower, 0), skewed(upper, 1)], axis=1)
    pieces = lax.all_to_all(pieces, "depth", 0, 0, tiled=True)
    return fold(pieces)


def solution(mesh):
    in_specs = (P("plane", None, "depth"), P(), P(), P(), P())
    out_specs = P(None, "plane", "depth")
    return jax.shard_map(body, mesh=mesh, in_specs=in_specs, out_specs=out_specs, check_vma=False)
```

```python
import functools
import math

import jax
import jax.numpy as jnp
import numpy as np
from jax import lax
from jax.experimental import pallas as pl
from jax.experimental.pallas import tpu as pltpu
from jax.sharding import PartitionSpec as P

INTERPRET = False
F32 = jnp.float32
BF16 = jnp.bfloat16
VMEM = pl.BlockSpec(memory_space=pltpu.VMEM)
SMEM = pl.BlockSpec(memory_space=pltpu.SMEM)

CX, NY, CZ, KNOTS, SHARE = 4, 512, 128, 16, 64
GROUP = CZ // CX
CHUNK = 64
WROWS = 16
HALF = 256
RING = 8
LIMIT = 36 << 20


def matmul(a, b):
    return jnp.dot(a, b, preferred_element_type=F32)


def along(table, index):
    numbers = lax.GatherDimensionNumbers(
        offset_dims=(),
        collapsed_slice_dims=(1,),
        start_index_map=(1,),
        operand_batching_dims=(0,),
        start_indices_batching_dims=(0,),
    )
    mode = lax.GatherScatterMode.PROMISE_IN_BOUNDS
    return lax.gather(table, index[..., None], numbers, slice_sizes=(1, 1), mode=mode)


def iota(shape, dim):
    return lax.broadcasted_iota(jnp.int32, shape, dim)


def prepare_kernel(
    vol_ref, transfer_ref, light_ref, bounds_ref, out_ref, tables_ref, limits_ref, window, square, sem
):
    planes = bounds_ref.shape[1] // CX
    column = CX * (lax.axis_index("plane") + lax.axis_index("depth"))
    start = pl.multiple_of(jnp.minimum((column // 8) * 8, planes * CX - 16), 8)
    copy = pltpu.make_async_copy(bounds_ref.at[:, pl.ds(start, 16), :], window, sem)
    copy.start()
    lane = iota((8, CZ), 1)
    for x in range(CX):
        packed = jnp.zeros((8, CZ), F32)
        for j in range(NY // 8):
            row = vol_ref[x, 8 * j : 8 * j + 8, :]
            moved = pltpu.roll(row, 2 * j, 1) if j else row
            keep = (lane == 2 * j) | (lane == (2 * j - 1) % CZ)
            packed = jnp.where(keep, moved, packed)
        out_ref[x] = packed
    square[...] = jnp.zeros_like(square)
    square[0:4, 0:KNOTS] = transfer_ref[...]
    knots = square[...]
    step = jnp.where(lane < KNOTS - 1, pltpu.roll(knots, CZ - 1, 1) - knots, 0.0)
    scale = jnp.where(iota((8, CZ), 0) == 3, -(2.0 / 1024) * math.log2(math.e), 1.0)
    tables_ref[0] = (knots - lane.astype(F32) * step) * scale
    tables_ref[1] = step * scale
    tables_ref[2] = jnp.zeros((8, CZ), F32)
    for axis in range(3):
        tables_ref[2, axis : axis + 1] = jnp.broadcast_to(light_ref[axis] * 0.7, (1, CZ))
    copy.wait()
    base = lax.axis_index("depth") * CZ
    turn = 16 - jnp.minimum(column - start, 15)
    ends = jnp.clip(window[...] - base, 0, CZ).astype(F32)
    first = pltpu.roll(ends[0], turn, 0)[0:8]
    last = pltpu.roll(ends[1], turn, 0)[0:8]
    limits = jnp.concatenate(
        [first, last, jnp.ones((1, NY), F32), jnp.zeros((CZ - 17, NY), F32)], axis=0
    )
    limits_ref[...] = limits.T.astype(BF16)


def prepare(volume, transfer, light, ray_bounds):
    return pl.pallas_call(
        prepare_kernel,
        out_shape=(
            jax.ShapeDtypeStruct((CX, 8, CZ), F32),
            jax.ShapeDtypeStruct((3, 8, CZ), F32),
            jax.ShapeDtypeStruct((NY, CZ), BF16),
        ),
        in_specs=[VMEM, VMEM, SMEM, pl.BlockSpec(memory_space=pltpu.HBM)],
        out_specs=(VMEM, VMEM, VMEM),
        scratch_shapes=[
            pltpu.VMEM((2, 16, NY), jnp.int32),
            pltpu.VMEM((8, CZ), F32),
            pltpu.SemaphoreType.DMA,
        ],
        compiler_params=pltpu.CompilerParams(vmem_limit_bytes=LIMIT),
        name="prepare",
        interpret=INTERPRET,
    )(volume, transfer.T, light, ray_bounds)


def constants():
    src = np.arange(2 * CZ)[:, None] % CZ
    lane = np.arange(2 * CZ)[None, :]
    dst = lane % CZ
    before = (src < dst) | ((src == dst) & (lane >= CZ))
    prefix = (src // GROUP == dst // GROUP) & before
    row = np.arange(CZ)[None, :, None]
    z = np.arange(CZ)[None, None, :]
    pixel = np.arange(CX)[:, None, None] + z // GROUP
    ahead = np.where(row == pixel, -1.0, np.where(row == 16, z + 0.5, 0.0))
    behind = np.where(row == pixel + 8, 1.0, np.where(row == 16, -(z + 0.5), 0.0))
    select = np.concatenate([ahead, behind], axis=2)
    row = np.arange(8 * CZ)[None, :, None]
    group = (row % CZ) // GROUP
    place = (group * 4 + row // (2 * CZ)) * 8 + np.arange(CX)[:, None, None] + group
    gather = np.arange(CZ)[None, None, :] == place
    return [jnp.asarray(np.asarray(a, np.float32), BF16) for a in (prefix, select, gather)]


def render_kernel(
    cells,
    vol_ref, plane_even_ref, plane_odd_ref, depth_even_ref, depth_odd_ref,
    resample_ref, tables_ref, limits_ref,
    prefix_ref, select_ref, gather_ref,
    image_ref,
    total, *buffers,
):
    lane8 = iota((8, CZ), 1)
    tables = [
        [jnp.broadcast_to(tables_ref[i, c : c + 1], (8, CZ)) for c in range(4)] for i in range(2)
    ]
    light0, light1, light2 = (
        jnp.broadcast_to(tables_ref[2, c : c + 1], (8, CZ)) for c in range(3)
    )
    plane_odd = lax.axis_index("plane") % 2 == 1
    depth_odd = lax.axis_index("depth") % 2 == 1
    lane = iota((CHUNK, CZ), 1)
    each = [[buffer.at[x] for buffer in buffers] for x in range(CX)]
    packed = {
        x: jnp.where(
            lane8 % 2 == 0,
            pltpu.roll(jnp.where(depth_odd, depth_even_ref[x], depth_odd_ref[x]), 1, 1),
            pltpu.roll(jnp.where(depth_odd, depth_odd_ref[x], depth_even_ref[x]), CZ - 1, 1),
        )
        for x in cells
    }

    def beside(x, here):
        if x < 0:
            return jnp.where(plane_odd, plane_even_ref[here, :], plane_odd_ref[here, :])
        if x == CX:
            return jnp.where(plane_odd, plane_odd_ref[here, :], plane_even_ref[here, :])
        return vol_ref[x, here, :]

    def differences(x, chunk):
        fields = each[x][0]
        r0 = chunk * CHUNK
        here = pl.ds(r0, CHUNK)
        f = vol_ref[x, here, :]
        below = beside(x - 1, here)
        above = beside(x + 1, here)
        blank = jnp.zeros((1, CZ), F32)
        if r0 == 0:
            prev = jnp.concatenate([blank, vol_ref[x, 0 : CHUNK - 1, :]], axis=0)
        else:
            prev = vol_ref[x, r0 - 1 : r0 + CHUNK - 1, :]
        if r0 + CHUNK == NY:
            following = jnp.concatenate([vol_ref[x, r0 + 1 : NY, :], blank], axis=0)
        else:
            following = vol_ref[x, r0 + 1 : r0 + CHUNK + 1, :]
        ends = jnp.concatenate(
            [
                pltpu.roll(packed[x], (CZ - 2 * j) % CZ, 1) if j else packed[x]
                for j in range(r0 // 8, (r0 + CHUNK) // 8)
            ],
            axis=0,
        )
        front = jnp.where(lane == 0, ends, pltpu.roll(f, 1, 1))
        back = jnp.where(lane == CZ - 1, ends, pltpu.roll(f, CZ - 1, 1))
        fields[here, 0:CZ] = f.astype(BF16)
        fields[here, CZ : 2 * CZ] = (above - below).astype(BF16)
        fields[here, 2 * CZ : 3 * CZ] = (following - prev).astype(BF16)
        fields[here, 3 * CZ : 4 * CZ] = (back - front).astype(BF16)

    def resampled(x, window):
        fields, samples = each[x][:2]
        first, last, k0 = ((0, 192, 0), (192, 320, 128), (320, 512, 256))[window]
        samples[first:last, :] = matmul(
            resample_ref[first:last, k0 : k0 + 256], fields[k0 : k0 + 256, :]
        )

    def distances(x):
        each[x][5][...] = matmul(limits_ref[...], select_ref[x])

    def classify(x, chunk):
        _, samples, colors, parts, _, masks = each[x]
        for row in range(chunk * CHUNK, (chunk + 1) * CHUNK, 8):
            here = pl.ds(row, 8)
            d = samples[here, 0:CZ]
            gx = samples[here, CZ : 2 * CZ]
            gy = samples[here, 2 * CZ : 3 * CZ]
            gz = samples[here, 3 * CZ : 4 * CZ]
            t = jnp.clip(d * 3.0 + 7.5, 0.0, KNOTS - 1.0)
            knot = t.astype(jnp.int32)

            def lookup(channel):
                return along(tables[0][channel], knot) + t * along(tables[1][channel], knot)

            lit = jnp.abs(gx * light0 + gy * light1 + gz * light2)
            lit = 0.3 + lit * lax.rsqrt(gx * gx + gy * gy + gz * gz + 4.0)
            inside = jnp.minimum(masks[here, 0:CZ], masks[here, CZ : 2 * CZ]) > 0.0
            tau = jnp.where(inside, lookup(3), 0.0)
            high = tau.astype(BF16)
            parts[here, 6 * CZ : 7 * CZ] = high
            parts[here, 7 * CZ : 8 * CZ] = (tau - high.astype(F32)).astype(BF16)
            for channel in range(3):
                colors[here, channel * CZ : (channel + 1) * CZ] = lookup(channel) * lit

    def depths(x, half):
        here = pl.ds(half * HALF, HALF)
        each[x][4][here, :] = matmul(each[x][3][here, 6 * CZ :], prefix_ref[...])

    def weigh(x, chunk):
        _, _, colors, parts, sums, _ = each[x]
        for row in range(chunk * CHUNK, (chunk + 1) * CHUNK, WROWS):
            here = pl.ds(row, WROWS)
            weight = jnp.exp2(sums[here, 0:CZ]) - jnp.exp2(sums[here, CZ : 2 * CZ])
            for channel in range(3):
                value = weight * colors[here, channel * CZ : (channel + 1) * CZ]
                high = value.astype(BF16)
                parts[here, 2 * channel * CZ : (2 * channel + 1) * CZ] = high
                parts[here, (2 * channel + 1) * CZ : (2 * channel + 2) * CZ] = (
                    value - high.astype(F32)
                ).astype(BF16)

    def gathered(x, half):
        here = pl.ds(half * HALF, HALF)
        part = matmul(each[x][3][here, :], gather_ref[x])
        if x == cells[0]:
            total[here, :] = part
        else:
            total[here, :] += part

    count = NY // CHUNK
    middle = count // 2
    for step in range(-1, len(cells) + 1):
        now = cells[step] if 0 <= step < len(cells) else None
        after = cells[step + 1] if step + 1 < len(cells) else None
        past = cells[step - 1] if step > 0 else None
        for chunk in range(count):
            if now is not None:
                classify(now, chunk)
            if after is not None:
                differences(after, chunk)
            if chunk >= middle and now is not None:
                weigh(now, chunk - middle)
            if chunk < middle and past is not None:
                weigh(past, chunk + middle)
            if chunk == middle - 1:
                if now is not None:
                    depths(now, 0)
                if past is not None:
                    gathered(past, 1)
                if after is not None:
                    resampled(after, 0)
            if chunk == middle + 1 and after is not None:
                resampled(after, 1)
        if now is not None:
            depths(now, 1)
            gathered(now, 0)
        if after is not None:
            resampled(after, 2)
            distances(after)

    image = total[...].T
    depth = jnp.zeros((8, NY), F32)
    color = [jnp.zeros((8, NY), F32) for _ in range(3)]
    for group in range(CX):
        through = jnp.exp2(depth)
        for channel in range(3):
            at = (group * 4 + channel) * 8
            color[channel] = color[channel] + through * image[at : at + 8]
        at = (group * 4 + 3) * 8
        depth = depth + image[at : at + 8]
    planes = color + [depth]
    sub = iota((8, CZ), 0)
    lane = iota((8, CZ), 1)
    for m in range(NY // CZ):
        tile = [plane[:, m * CZ : (m + 1) * CZ] for plane in planes]
        turned = [pltpu.roll(part, 4, 0) for part in tile]
        for side, a, b in (
            (0, jnp.where(sub < 4, tile[0], turned[1]), jnp.where(sub < 4, tile[2], turned[3])),
            (1, jnp.where(sub < 4, turned[0], tile[1]), jnp.where(sub < 4, turned[2], tile[3])),
        ):
            image_ref[2 * m, side] = jnp.where(lane < SHARE, a, pltpu.roll(b, SHARE, 1))
            image_ref[2 * m + 1, side] = jnp.where(lane < SHARE, pltpu.roll(a, SHARE, 1), b)


def render(*operands):
    return pl.pallas_call(
        functools.partial(render_kernel, tuple(range(CX))),
        out_shape=jax.ShapeDtypeStruct((8, 2, 8, CZ), F32),
        in_specs=[VMEM] * 11,
        out_specs=VMEM,
        scratch_shapes=[pltpu.VMEM((NY, CZ), F32)]
        + [
            pltpu.VMEM((CX, NY, width * CZ), kind)
            for width, kind in ((4, BF16), (4, F32), (3, F32), (8, BF16), (2, F32), (2, F32))
        ],
        compiler_params=pltpu.CompilerParams(vmem_limit_bytes=LIMIT),
        name="render",
        interpret=INTERPRET,
    )(*operands)


def through(piece):
    sub = iota((8, CZ), 0)
    lane = iota((8, CZ), 1)
    depth = jnp.where(lane >= SHARE, piece, pltpu.roll(piece, SHARE, 1))
    return jnp.where(sub >= 4, depth, pltpu.roll(depth, 4, 0))


def over(front, back):
    is_depth = (iota((8, CZ), 0) >= 4) & (iota((8, CZ), 1) >= SHARE)
    passed = jnp.exp2(through(front))
    return front + jnp.where(is_depth, 1.0, passed) * back


def small_call(kernel, shapes, name, *operands):
    return pl.pallas_call(
        kernel,
        out_shape=tuple(jax.ShapeDtypeStruct(shape, F32) for shape in shapes),
        in_specs=[VMEM] * len(operands),
        out_specs=(VMEM,) * len(shapes),
        compiler_params=pltpu.CompilerParams(vmem_limit_bytes=LIMIT),
        name=name,
        interpret=INTERPRET,
    )(*operands)


def merge_kernel(pieces_ref, ring_ref, last_ref):
    place = lax.axis_index("plane") % RING
    count = pieces_ref.shape[0]
    ring_ref[place] = pieces_ref[0, 0]
    for j in range(1, count):
        ring_ref[(place + j) % RING] = over(pieces_ref[j - 1, 1], pieces_ref[j, 0])
    last_ref[...] = pieces_ref[count - 1, 1]


def pass_kernel(ring_ref, last_ref, own_ref, next_ref):
    place = lax.axis_index("plane") % RING
    own = ring_ref[place]
    following = None
    for j in range(1, RING):
        piece = ring_ref[(place - j + RING) % RING]
        mine = jnp.where(j <= place, 1.0, 0.0)
        own = over(own, piece * mine)
        other = piece * (1.0 - mine)
        following = other if following is None else over(following, other)
    own_ref[...] = own
    next_ref[...] = over(following, last_ref[...])


def finish_kernel(front_ref, back_ref, out_ref):
    image = over(front_ref[...], back_ref[...])
    is_depth = (iota((8, CZ), 0) >= 4) & (iota((8, CZ), 1) >= SHARE)
    image = jnp.where(is_depth, 1.0 - jnp.exp2(image), image)
    turned = pltpu.roll(image, SHARE, 1)
    out_ref[0] = image[0:4, 0:SHARE]
    out_ref[1] = image[4:8, 0:SHARE]
    out_ref[2] = turned[0:4, 0:SHARE]
    out_ref[3] = turned[4:8, 0:SHARE]


def body(volume, resample, transfer, light, ray_bounds):
    planes = lax.axis_size("plane")
    depths = lax.axis_size("depth")

    def exchanged(value, axis, first):
        pairs = []
        for i in range(first, lax.axis_size(axis) - 1, 2):
            pairs += [(i, i + 1), (i + 1, i)]
        return lax.ppermute(value, axis, pairs)

    odd = lax.axis_index("plane") % 2
    outward = lax.dynamic_index_in_dim(volume, (CX - 1) * (1 - odd), 0, keepdims=False)
    inward = lax.dynamic_index_in_dim(volume, (CX - 1) * odd, 0, keepdims=False)
    plane_even = exchanged(outward, "plane", 0)
    plane_odd = exchanged(inward, "plane", 1)
    faces, tables, limits = prepare(volume, transfer, light, ray_bounds)
    depth_even = exchanged(faces, "depth", 0)
    depth_odd = exchanged(faces, "depth", 1)
    images = render(
        volume, plane_even, plane_odd, depth_even, depth_odd,
        resample, tables, limits, *constants(),
    )

    tile = (8, CZ)
    pieces = lax.all_to_all(images, "depth", 0, 0, tiled=True)
    ring, last = small_call(merge_kernel, [(RING,) + tile, tile], "merge", pieces)
    groups = [
        [(row * RING + place) * depths + d for place in range(RING)]
        for row in range(planes // RING)
        for d in range(depths)
    ]
    ring = lax.all_to_all(
        ring, ("plane", "depth"), 0, 0, tiled=True, axis_index_groups=groups
    )
    own, following = small_call(pass_kernel, [tile, tile], "pass", ring, last)
    behind = lax.ppermute(following, "plane", [(p, p + RING) for p in range(planes - RING)])
    return small_call(finish_kernel, [(4, CX, SHARE)], "finish", own, behind)[0]


def solution(mesh):
    in_specs = (P("plane", None, "depth"), P(), P(), P(), P())
    out_specs = P(None, "plane", "depth")
    return jax.shard_map(body, mesh=mesh, in_specs=in_specs, out_specs=out_specs, check_vma=False)
```

```python
import functools
import math

import jax
import jax.numpy as jnp
import numpy as np
from jax import lax
from jax.experimental import pallas as pl
from jax.experimental.pallas import tpu as pltpu
from jax.sharding import PartitionSpec as P

INTERPRET = False
F32 = jnp.float32
BF16 = jnp.bfloat16
VMEM = pl.BlockSpec(memory_space=pltpu.VMEM)
SMEM = pl.BlockSpec(memory_space=pltpu.SMEM)

CX, NY, CZ, KNOTS, SHARE = 4, 512, 128, 16, 64
GROUP = CZ // CX
CHUNK = 64
WROWS = 16
HALF = 256
LIMIT = 14 << 20
INNER, OUTER = (1, 2), (0, 3)


def matmul(a, b):
    return jnp.dot(a, b, preferred_element_type=F32)


def along(table, index):
    numbers = lax.GatherDimensionNumbers(
        offset_dims=(),
        collapsed_slice_dims=(1,),
        start_index_map=(1,),
        operand_batching_dims=(0,),
        start_indices_batching_dims=(0,),
    )
    mode = lax.GatherScatterMode.PROMISE_IN_BOUNDS
    return lax.gather(table, index[..., None], numbers, slice_sizes=(1, 1), mode=mode)


def iota(shape, dim):
    return lax.broadcasted_iota(jnp.int32, shape, dim)


def faces_kernel(vol_ref, out_ref):
    lane = iota((8, CZ), 1)
    for x in range(CX):
        packed = jnp.zeros((8, CZ), F32)
        for j in range(NY // 8):
            row = vol_ref[x, 8 * j : 8 * j + 8, :]
            moved = pltpu.roll(row, 2 * j, 1) if j else row
            keep = (lane == 2 * j) | (lane == (2 * j - 1) % CZ)
            packed = jnp.where(keep, moved, packed)
        out_ref[x] = packed


def pack_faces(volume):
    return pl.pallas_call(
        faces_kernel,
        out_shape=jax.ShapeDtypeStruct((CX, 8, CZ), F32),
        in_specs=[VMEM],
        out_specs=VMEM,
        compiler_params=pltpu.CompilerParams(vmem_limit_bytes=LIMIT),
        name="faces",
        interpret=INTERPRET,
    )(volume)


def prepare_kernel(
    transfer_ref, light_ref, bounds_ref, tables_ref, limits_ref, window, square, sem
):
    planes = bounds_ref.shape[1] // CX
    column = CX * (lax.axis_index("plane") + lax.axis_index("depth"))
    start = pl.multiple_of(jnp.minimum((column // 8) * 8, planes * CX - 16), 8)
    copy = pltpu.make_async_copy(bounds_ref.at[:, pl.ds(start, 16), :], window, sem)
    copy.start()
    lane = iota((8, CZ), 1)
    square[...] = jnp.zeros_like(square)
    square[0:4, 0:KNOTS] = transfer_ref[...]
    knots = square[...]
    step = jnp.where(lane < KNOTS - 1, pltpu.roll(knots, CZ - 1, 1) - knots, 0.0)
    scale = jnp.where(iota((8, CZ), 0) == 3, -(2.0 / 1024) * math.log2(math.e), 1.0)
    tables_ref[0] = (knots - lane.astype(F32) * step) * scale
    tables_ref[1] = step * scale
    tables_ref[2] = jnp.zeros((8, CZ), F32)
    for axis in range(3):
        tables_ref[2, axis : axis + 1] = jnp.broadcast_to(light_ref[axis] * 0.7, (1, CZ))
    copy.wait()
    base = lax.axis_index("depth") * CZ
    turn = 16 - jnp.minimum(column - start, 15)
    ends = jnp.clip(window[...] - base, 0, CZ).astype(F32)
    first = pltpu.roll(ends[0], turn, 0)[0:8]
    last = pltpu.roll(ends[1], turn, 0)[0:8]
    limits = jnp.concatenate(
        [first, last, jnp.ones((1, NY), F32), jnp.zeros((CZ - 17, NY), F32)], axis=0
    )
    limits_ref[...] = limits.T.astype(BF16)


def prepare(transfer, light, ray_bounds):
    return pl.pallas_call(
        prepare_kernel,
        out_shape=(
            jax.ShapeDtypeStruct((3, 8, CZ), F32),
            jax.ShapeDtypeStruct((NY, CZ), BF16),
        ),
        in_specs=[VMEM, SMEM, pl.BlockSpec(memory_space=pltpu.HBM)],
        out_specs=(VMEM, VMEM),
        scratch_shapes=[
            pltpu.VMEM((2, 16, NY), jnp.int32),
            pltpu.VMEM((8, CZ), F32),
            pltpu.SemaphoreType.DMA,
        ],
        compiler_params=pltpu.CompilerParams(vmem_limit_bytes=LIMIT),
        name="prepare",
        interpret=INTERPRET,
    )(transfer.T, light, ray_bounds)


def constants():
    src = np.arange(2 * CZ)[:, None] % CZ
    lane = np.arange(2 * CZ)[None, :]
    dst = lane % CZ
    before = (src < dst) | ((src == dst) & (lane >= CZ))
    prefix = (src // GROUP == dst // GROUP) & before
    row = np.arange(CZ)[None, :, None]
    z = np.arange(CZ)[None, None, :]
    pixel = np.arange(CX)[:, None, None] + z // GROUP
    ahead = np.where(row == pixel, -1.0, np.where(row == 16, z + 0.5, 0.0))
    behind = np.where(row == pixel + 8, 1.0, np.where(row == 16, -(z + 0.5), 0.0))
    select = np.concatenate([ahead, behind], axis=2)
    row = np.arange(8 * CZ)[None, :, None]
    group = (row % CZ) // GROUP
    place = (group * 4 + row // (2 * CZ)) * 8 + np.arange(CX)[:, None, None] + group
    gather = np.arange(CZ)[None, None, :] == place
    square = np.concatenate([prefix, select.reshape(CX * CZ, 2 * CZ)], axis=0)
    return [jnp.asarray(np.asarray(a, np.float32), BF16) for a in (square, gather)]


def inner_kernel(
    vol_ref, depth_even_ref, depth_odd_ref, resample_ref, tables_ref, limits_ref,
    square_ref, gather_ref,
    total_ref, *buffers,
):
    accumulate(
        INNER, vol_ref, None, None, depth_even_ref, depth_odd_ref,
        resample_ref, tables_ref, limits_ref, square_ref, gather_ref,
        None, total_ref, buffers,
    )


def outer_kernel(
    vol_ref, plane_even_ref, plane_odd_ref, depth_even_ref, depth_odd_ref,
    resample_ref, tables_ref, limits_ref, square_ref, gather_ref, inner_ref,
    lower_ref, upper_ref, total, *buffers,
):
    accumulate(
        OUTER, vol_ref, plane_even_ref, plane_odd_ref, depth_even_ref, depth_odd_ref,
        resample_ref, tables_ref, limits_ref, square_ref, gather_ref,
        inner_ref, total, buffers,
    )
    compose(total, lower_ref, upper_ref)


def accumulate(
    cells, vol_ref, plane_even_ref, plane_odd_ref, depth_even_ref, depth_odd_ref,
    resample_ref, tables_ref, limits_ref, square_ref, gather_ref,
    earlier, total, buffers,
):
    lane8 = iota((8, CZ), 1)
    tables = [
        [jnp.broadcast_to(tables_ref[i, c : c + 1], (8, CZ)) for c in range(4)] for i in range(2)
    ]
    light0, light1, light2 = (
        jnp.broadcast_to(tables_ref[2, c : c + 1], (8, CZ)) for c in range(3)
    )
    plane_odd = lax.axis_index("plane") % 2 == 1
    depth_odd = lax.axis_index("depth") % 2 == 1
    lane = iota((CHUNK, CZ), 1)
    each = {x: [buffer.at[i] for buffer in buffers] for i, x in enumerate(cells)}
    packed = {
        x: jnp.where(
            lane8 % 2 == 0,
            pltpu.roll(jnp.where(depth_odd, depth_even_ref[x], depth_odd_ref[x]), 1, 1),
            pltpu.roll(jnp.where(depth_odd, depth_odd_ref[x], depth_even_ref[x]), CZ - 1, 1),
        )
        for x in cells
    }

    def beside(x, here):
        if x < 0:
            return jnp.where(plane_odd, plane_even_ref[here, :], plane_odd_ref[here, :])
        if x == CX:
            return jnp.where(plane_odd, plane_odd_ref[here, :], plane_even_ref[here, :])
        return vol_ref[x, here, :]

    def differences(x, chunk):
        fields = each[x][0]
        r0 = chunk * CHUNK
        here = pl.ds(r0, CHUNK)
        f = vol_ref[x, here, :]
        below = beside(x - 1, here)
        above = beside(x + 1, here)
        blank = jnp.zeros((1, CZ), F32)
        if r0 == 0:
            prev = jnp.concatenate([blank, vol_ref[x, 0 : CHUNK - 1, :]], axis=0)
        else:
            prev = vol_ref[x, r0 - 1 : r0 + CHUNK - 1, :]
        if r0 + CHUNK == NY:
            following = jnp.concatenate([vol_ref[x, r0 + 1 : NY, :], blank], axis=0)
        else:
            following = vol_ref[x, r0 + 1 : r0 + CHUNK + 1, :]
        ends = jnp.concatenate(
            [
                pltpu.roll(packed[x], (CZ - 2 * j) % CZ, 1) if j else packed[x]
                for j in range(r0 // 8, (r0 + CHUNK) // 8)
            ],
            axis=0,
        )
        front = jnp.where(lane == 0, ends, pltpu.roll(f, 1, 1))
        back = jnp.where(lane == CZ - 1, ends, pltpu.roll(f, CZ - 1, 1))
        fields[here, 0:CZ] = f.astype(BF16)
        fields[here, CZ : 2 * CZ] = (above - below).astype(BF16)
        fields[here, 2 * CZ : 3 * CZ] = (following - prev).astype(BF16)
        fields[here, 3 * CZ : 4 * CZ] = (back - front).astype(BF16)

    def resampled(x, window):
        fields, samples = each[x][:2]
        first, last, k0 = ((0, 192, 0), (192, 320, 128), (320, 512, 256))[window]
        samples[first:last, :] = matmul(
            resample_ref[first:last, k0 : k0 + 256], fields[k0 : k0 + 256, :]
        )

    def distances(x):
        each[x][5][...] = matmul(limits_ref[...], square_ref[(2 + x) * CZ : (3 + x) * CZ, :])

    def classify(x, chunk):
        _, samples, colors, parts, _, masks = each[x]
        for row in range(chunk * CHUNK, (chunk + 1) * CHUNK, 8):
            here = pl.ds(row, 8)
            d = samples[here, 0:CZ]
            gx = samples[here, CZ : 2 * CZ]
            gy = samples[here, 2 * CZ : 3 * CZ]
            gz = samples[here, 3 * CZ : 4 * CZ]
            t = jnp.clip(d * 3.0 + 7.5, 0.0, KNOTS - 1.0)
            knot = t.astype(jnp.int32)

            def lookup(channel):
                return along(tables[0][channel], knot) + t * along(tables[1][channel], knot)

            lit = jnp.abs(gx * light0 + gy * light1 + gz * light2)
            lit = 0.3 + lit * lax.rsqrt(gx * gx + gy * gy + gz * gz + 4.0)
            inside = jnp.minimum(masks[here, 0:CZ], masks[here, CZ : 2 * CZ]) > 0.0
            tau = jnp.where(inside, lookup(3), 0.0)
            high = tau.astype(BF16)
            parts[here, 6 * CZ : 7 * CZ] = high
            parts[here, 7 * CZ : 8 * CZ] = (tau - high.astype(F32)).astype(BF16)
            for channel in range(3):
                colors[here, channel * CZ : (channel + 1) * CZ] = lookup(channel) * lit

    def depths(x, half):
        here = pl.ds(half * HALF, HALF)
        each[x][4][here, :] = matmul(each[x][3][here, 6 * CZ :], square_ref[0 : 2 * CZ, :])

    def weigh(x, chunk):
        _, _, colors, parts, sums, _ = each[x]
        for row in range(chunk * CHUNK, (chunk + 1) * CHUNK, WROWS):
            here = pl.ds(row, WROWS)
            weight = jnp.exp2(sums[here, 0:CZ]) - jnp.exp2(sums[here, CZ : 2 * CZ])
            for channel in range(3):
                value = weight * colors[here, channel * CZ : (channel + 1) * CZ]
                high = value.astype(BF16)
                parts[here, 2 * channel * CZ : (2 * channel + 1) * CZ] = high
                parts[here, (2 * channel + 1) * CZ : (2 * channel + 2) * CZ] = (
                    value - high.astype(F32)
                ).astype(BF16)

    def gathered(x, half):
        here = pl.ds(half * HALF, HALF)
        part = matmul(each[x][3][here, :], gather_ref[x])
        if x == cells[0]:
            total[here, :] = part if earlier is None else earlier[here, :] + part
        else:
            total[here, :] += part

    count = NY // CHUNK
    middle = count // 2
    for step in range(-1, len(cells) + 1):
        now = cells[step] if 0 <= step < len(cells) else None
        after = cells[step + 1] if step + 1 < len(cells) else None
        past = cells[step - 1] if step > 0 else None
        for chunk in range(count):
            if now is not None:
                classify(now, chunk)
            if after is not None:
                differences(after, chunk)
            if chunk >= middle and now is not None:
                weigh(now, chunk - middle)
            if chunk < middle and past is not None:
                weigh(past, chunk + middle)
            if chunk == middle - 1:
                if now is not None:
                    depths(now, 0)
                if past is not None:
                    gathered(past, 1)
                if after is not None:
                    resampled(after, 0)
            if chunk == middle + 1 and after is not None:
                resampled(after, 1)
        if now is not None:
            depths(now, 1)
            gathered(now, 0)
        if after is not None:
            resampled(after, 2)
            distances(after)


def compose(total, lower_ref, upper_ref):
    image = total[...].T
    depth = jnp.zeros((8, NY), F32)
    color = [jnp.zeros((8, NY), F32) for _ in range(3)]
    for group in range(CX):
        through = jnp.exp2(depth)
        for channel in range(3):
            at = (group * 4 + channel) * 8
            color[channel] = color[channel] + through * image[at : at + 8]
        at = (group * 4 + 3) * 8
        depth = depth + image[at : at + 8]
    planes = color + [depth]
    sub = iota((8, CZ), 0)
    lane = iota((8, CZ), 1)
    for m in range(NY // CZ):
        tile = [plane[:, m * CZ : (m + 1) * CZ] for plane in planes]
        turned = [pltpu.roll(part, 4, 0) for part in tile]
        for ref, a, b in (
            (lower_ref, jnp.where(sub < 4, tile[0], turned[1]), jnp.where(sub < 4, tile[2], turned[3])),
            (upper_ref, jnp.where(sub < 4, turned[0], tile[1]), jnp.where(sub < 4, turned[2], tile[3])),
        ):
            ref[2 * m] = jnp.where(lane < SHARE, a, pltpu.roll(b, SHARE, 1))
            ref[2 * m + 1] = jnp.where(lane < SHARE, pltpu.roll(a, SHARE, 1), b)


def buffers():
    return [
        pltpu.VMEM((2, NY, width * CZ), kind)
        for width, kind in ((4, BF16), (4, F32), (3, F32), (8, BF16), (2, F32), (2, F32))
    ]


def render_inner(*operands):
    return pl.pallas_call(
        inner_kernel,
        out_shape=jax.ShapeDtypeStruct((NY, CZ), F32),
        in_specs=[VMEM] * len(operands),
        out_specs=VMEM,
        scratch_shapes=buffers(),
        compiler_params=pltpu.CompilerParams(vmem_limit_bytes=LIMIT),
        name="inner",
        interpret=INTERPRET,
    )(*operands)


def render_outer(*operands):
    block = jax.ShapeDtypeStruct((8, 8, CZ), F32)
    return pl.pallas_call(
        outer_kernel,
        out_shape=(block, block),
        in_specs=[VMEM] * len(operands),
        out_specs=(VMEM, VMEM),
        scratch_shapes=[pltpu.VMEM((NY, CZ), F32)] + buffers(),
        compiler_params=pltpu.CompilerParams(vmem_limit_bytes=LIMIT),
        name="outer",
        interpret=INTERPRET,
    )(*operands)


def fold_kernel(pieces_ref, out_ref):
    sub = iota((8, CZ), 0)
    lane = iota((8, CZ), 1)
    color = jnp.zeros((8, CZ), F32)
    depth = jnp.zeros((8, CZ), F32)
    for d in range(pieces_ref.shape[0]):
        for side in range(2):
            piece = pieces_ref[d, side]
            own = jnp.where(lane >= SHARE, piece, pltpu.roll(piece, SHARE, 1))
            own = jnp.where(sub >= 4, own, pltpu.roll(own, 4, 0))
            color = color + jnp.exp2(depth) * piece
            depth = depth + own
    opacity = 1.0 - jnp.exp2(depth)
    color = jnp.where((sub >= 4) & (lane >= SHARE), opacity, color)
    turned = pltpu.roll(color, SHARE, 1)
    out_ref[0] = color[0:4, 0:SHARE]
    out_ref[1] = color[4:8, 0:SHARE]
    out_ref[2] = turned[0:4, 0:SHARE]
    out_ref[3] = turned[4:8, 0:SHARE]


def fold(pieces):
    return pl.pallas_call(
        fold_kernel,
        out_shape=jax.ShapeDtypeStruct((4, CX, SHARE), F32),
        in_specs=[VMEM],
        out_specs=VMEM,
        compiler_params=pltpu.CompilerParams(vmem_limit_bytes=LIMIT),
        name="fold",
        interpret=INTERPRET,
    )(pieces)


def body(volume, resample, transfer, light, ray_bounds):
    planes = lax.axis_size("plane")
    depths = lax.axis_size("depth")

    def exchanged(value, axis, first):
        pairs = []
        for i in range(first, lax.axis_size(axis) - 1, 2):
            pairs += [(i, i + 1), (i + 1, i)]
        return lax.ppermute(value, axis, pairs)

    odd = lax.axis_index("plane") % 2
    outward = lax.dynamic_index_in_dim(volume, (CX - 1) * (1 - odd), 0, keepdims=False)
    inward = lax.dynamic_index_in_dim(volume, (CX - 1) * odd, 0, keepdims=False)
    plane_even = exchanged(outward, "plane", 0)
    plane_odd = exchanged(inward, "plane", 1)
    faces = pack_faces(volume)
    depth_even = exchanged(faces, "depth", 0)
    depth_odd = exchanged(faces, "depth", 1)
    tables, limits = prepare(transfer, light, ray_bounds)
    shared = (resample, tables, limits, *constants())
    inner = render_inner(volume, depth_even, depth_odd, *shared)
    lower, upper = render_outer(
        volume, plane_even, plane_odd, depth_even, depth_odd, *shared, inner
    )

    def skewed(value, extra):
        pairs = [
            (p * depths + d, (p + d + extra) * depths + d)
            for p in range(planes)
            for d in range(depths)
            if p + d + extra < planes
        ]
        return lax.ppermute(value, ("plane", "depth"), pairs)

    pieces = jnp.stack([skewed(lower, 0), skewed(upper, 1)], axis=1)
    pieces = lax.all_to_all(pieces, "depth", 0, 0, tiled=True)
    return fold(pieces)


def solution(mesh):
    in_specs = (P("plane", None, "depth"), P(), P(), P(), P())
    out_specs = P(None, "plane", "depth")
    return jax.shard_map(body, mesh=mesh, in_specs=in_specs, out_specs=out_specs, check_vma=False)
```

```python
import functools
import math

import jax
import jax.numpy as jnp
import numpy as np
from jax import lax
from jax.experimental import pallas as pl
from jax.experimental.pallas import tpu as pltpu
from jax.sharding import PartitionSpec as P

INTERPRET = False
F32 = jnp.float32
BF16 = jnp.bfloat16
VMEM = pl.BlockSpec(memory_space=pltpu.VMEM)
SMEM = pl.BlockSpec(memory_space=pltpu.SMEM)

CX, NY, CZ, KNOTS, SHARE = 4, 512, 128, 16, 64
GROUP = CZ // CX
CHUNK = 64
WROWS = 16
HALF = 256
LIMIT = 14 << 20
INNER, OUTER = (1, 2), (0, 3)


def matmul(a, b):
    return jnp.dot(a, b, preferred_element_type=F32)


def along(table, index):
    numbers = lax.GatherDimensionNumbers(
        offset_dims=(),
        collapsed_slice_dims=(1,),
        start_index_map=(1,),
        operand_batching_dims=(0,),
        start_indices_batching_dims=(0,),
    )
    mode = lax.GatherScatterMode.PROMISE_IN_BOUNDS
    return lax.gather(table, index[..., None], numbers, slice_sizes=(1, 1), mode=mode)


def iota(shape, dim):
    return lax.broadcasted_iota(jnp.int32, shape, dim)


def faces_kernel(vol_ref, out_ref):
    lane = iota((8, CZ), 1)
    for x in range(CX):
        packed = jnp.zeros((8, CZ), F32)
        for j in range(NY // 8):
            row = vol_ref[x, 8 * j : 8 * j + 8, :]
            moved = pltpu.roll(row, 2 * j, 1) if j else row
            keep = (lane == 2 * j) | (lane == (2 * j - 1) % CZ)
            packed = jnp.where(keep, moved, packed)
        out_ref[x] = packed


def pack_faces(volume):
    return pl.pallas_call(
        faces_kernel,
        out_shape=jax.ShapeDtypeStruct((CX, 8, CZ), F32),
        in_specs=[VMEM],
        out_specs=VMEM,
        compiler_params=pltpu.CompilerParams(vmem_limit_bytes=LIMIT),
        name="faces",
        interpret=INTERPRET,
    )(volume)


def prepare_kernel(
    transfer_ref, light_ref, bounds_ref, tables_ref, limits_ref, window, square, sem
):
    planes = bounds_ref.shape[1] // CX
    column = CX * (lax.axis_index("plane") + lax.axis_index("depth"))
    start = pl.multiple_of(jnp.minimum((column // 8) * 8, planes * CX - 16), 8)
    copy = pltpu.make_async_copy(bounds_ref.at[:, pl.ds(start, 16), :], window, sem)
    copy.start()
    lane = iota((8, CZ), 1)
    square[...] = jnp.zeros_like(square)
    square[0:4, 0:KNOTS] = transfer_ref[...]
    knots = square[...]
    step = jnp.where(lane < KNOTS - 1, pltpu.roll(knots, CZ - 1, 1) - knots, 0.0)
    scale = jnp.where(iota((8, CZ), 0) == 3, -(2.0 / 1024) * math.log2(math.e), 1.0)
    tables_ref[0] = (knots - lane.astype(F32) * step) * scale
    tables_ref[1] = step * scale
    tables_ref[2] = jnp.zeros((8, CZ), F32)
    for axis in range(3):
        tables_ref[2, axis : axis + 1] = jnp.broadcast_to(light_ref[axis] * 0.7, (1, CZ))
    copy.wait()
    base = lax.axis_index("depth") * CZ
    turn = 16 - jnp.minimum(column - start, 15)
    ends = jnp.clip(window[...] - base, 0, CZ).astype(F32)
    first = pltpu.roll(ends[0], turn, 0)[0:8]
    last = pltpu.roll(ends[1], turn, 0)[0:8]
    limits = jnp.concatenate(
        [first, last, jnp.ones((1, NY), F32), jnp.zeros((CZ - 17, NY), F32)], axis=0
    )
    limits_ref[...] = limits.T.astype(BF16)


def prepare(transfer, light, ray_bounds):
    return pl.pallas_call(
        prepare_kernel,
        out_shape=(
            jax.ShapeDtypeStruct((3, 8, CZ), F32),
            jax.ShapeDtypeStruct((NY, CZ), BF16),
        ),
        in_specs=[VMEM, SMEM, pl.BlockSpec(memory_space=pltpu.HBM)],
        out_specs=(VMEM, VMEM),
        scratch_shapes=[
            pltpu.VMEM((2, 16, NY), jnp.int32),
            pltpu.VMEM((8, CZ), F32),
            pltpu.SemaphoreType.DMA,
        ],
        compiler_params=pltpu.CompilerParams(vmem_limit_bytes=LIMIT),
        name="prepare",
        interpret=INTERPRET,
    )(transfer.T, light, pltpu.with_memory_space_constraint(ray_bounds, pltpu.HBM))


def constants():
    src = np.arange(2 * CZ)[:, None] % CZ
    lane = np.arange(2 * CZ)[None, :]
    dst = lane % CZ
    before = (src < dst) | ((src == dst) & (lane >= CZ))
    prefix = (src // GROUP == dst // GROUP) & before
    row = np.arange(CZ)[None, :, None]
    z = np.arange(CZ)[None, None, :]
    pixel = np.arange(CX)[:, None, None] + z // GROUP
    ahead = np.where(row == pixel, -1.0, np.where(row == 16, z + 0.5, 0.0))
    behind = np.where(row == pixel + 8, 1.0, np.where(row == 16, -(z + 0.5), 0.0))
    select = np.concatenate([ahead, behind], axis=2)
    row = np.arange(8 * CZ)[None, :, None]
    group = (row % CZ) // GROUP
    place = (group * 4 + row // (2 * CZ)) * 8 + np.arange(CX)[:, None, None] + group
    gather = np.arange(CZ)[None, None, :] == place
    square = np.concatenate([prefix, select.reshape(CX * CZ, 2 * CZ)], axis=0)
    return [jnp.asarray(np.asarray(a, np.float32), BF16) for a in (square, gather)]


def inner_kernel(
    vol_ref, depth_even_ref, depth_odd_ref, resample_ref, tables_ref, limits_ref,
    square_ref, gather_ref,
    total_ref, *buffers,
):
    accumulate(
        INNER, vol_ref, None, None, depth_even_ref, depth_odd_ref,
        resample_ref, tables_ref, limits_ref, square_ref, gather_ref,
        None, total_ref, buffers,
    )


def outer_kernel(
    vol_ref, plane_even_ref, plane_odd_ref, depth_even_ref, depth_odd_ref,
    resample_ref, tables_ref, limits_ref, square_ref, gather_ref, inner_ref,
    lower_ref, upper_ref, total, *buffers,
):
    accumulate(
        OUTER, vol_ref, plane_even_ref, plane_odd_ref, depth_even_ref, depth_odd_ref,
        resample_ref, tables_ref, limits_ref, square_ref, gather_ref,
        inner_ref, total, buffers,
    )
    compose(total, lower_ref, upper_ref)


def accumulate(
    cells, vol_ref, plane_even_ref, plane_odd_ref, depth_even_ref, depth_odd_ref,
    resample_ref, tables_ref, limits_ref, square_ref, gather_ref,
    earlier, total, buffers,
):
    lane8 = iota((8, CZ), 1)
    tables = [
        [jnp.broadcast_to(tables_ref[i, c : c + 1], (8, CZ)) for c in range(4)] for i in range(2)
    ]
    light0, light1, light2 = (
        jnp.broadcast_to(tables_ref[2, c : c + 1], (8, CZ)) for c in range(3)
    )
    plane_odd = lax.axis_index("plane") % 2 == 1
    depth_odd = lax.axis_index("depth") % 2 == 1
    lane = iota((CHUNK, CZ), 1)
    each = {x: [buffer.at[i] for buffer in buffers] for i, x in enumerate(cells)}
    packed = {
        x: jnp.where(
            lane8 % 2 == 0,
            pltpu.roll(jnp.where(depth_odd, depth_even_ref[x], depth_odd_ref[x]), 1, 1),
            pltpu.roll(jnp.where(depth_odd, depth_odd_ref[x], depth_even_ref[x]), CZ - 1, 1),
        )
        for x in cells
    }

    def beside(x, here):
        if x < 0:
            return jnp.where(plane_odd, plane_even_ref[here, :], plane_odd_ref[here, :])
        if x == CX:
            return jnp.where(plane_odd, plane_odd_ref[here, :], plane_even_ref[here, :])
        return vol_ref[x, here, :]

    def differences(x, chunk):
        fields = each[x][0]
        r0 = chunk * CHUNK
        here = pl.ds(r0, CHUNK)
        f = vol_ref[x, here, :]
        below = beside(x - 1, here)
        above = beside(x + 1, here)
        blank = jnp.zeros((1, CZ), F32)
        if r0 == 0:
            prev = jnp.concatenate([blank, vol_ref[x, 0 : CHUNK - 1, :]], axis=0)
        else:
            prev = vol_ref[x, r0 - 1 : r0 + CHUNK - 1, :]
        if r0 + CHUNK == NY:
            following = jnp.concatenate([vol_ref[x, r0 + 1 : NY, :], blank], axis=0)
        else:
            following = vol_ref[x, r0 + 1 : r0 + CHUNK + 1, :]
        ends = jnp.concatenate(
            [
                pltpu.roll(packed[x], (CZ - 2 * j) % CZ, 1) if j else packed[x]
                for j in range(r0 // 8, (r0 + CHUNK) // 8)
            ],
            axis=0,
        )
        front = jnp.where(lane == 0, ends, pltpu.roll(f, 1, 1))
        back = jnp.where(lane == CZ - 1, ends, pltpu.roll(f, CZ - 1, 1))
        fields[here, 0:CZ] = f.astype(BF16)
        fields[here, CZ : 2 * CZ] = (above - below).astype(BF16)
        fields[here, 2 * CZ : 3 * CZ] = (following - prev).astype(BF16)
        fields[here, 3 * CZ : 4 * CZ] = (back - front).astype(BF16)

    def resampled(x, window):
        fields, samples = each[x][:2]
        first, last, k0 = ((0, 192, 0), (192, 320, 128), (320, 512, 256))[window]
        samples[first:last, :] = matmul(
            resample_ref[first:last, k0 : k0 + 256], fields[k0 : k0 + 256, :]
        )

    def distances(x):
        each[x][5][...] = matmul(limits_ref[...], square_ref[(2 + x) * CZ : (3 + x) * CZ, :])

    def classify(x, chunk):
        _, samples, colors, parts, _, masks = each[x]
        for row in range(chunk * CHUNK, (chunk + 1) * CHUNK, 8):
            here = pl.ds(row, 8)
            d = samples[here, 0:CZ]
            gx = samples[here, CZ : 2 * CZ]
            gy = samples[here, 2 * CZ : 3 * CZ]
            gz = samples[here, 3 * CZ : 4 * CZ]
            t = jnp.clip(d * 3.0 + 7.5, 0.0, KNOTS - 1.0)
            knot = t.astype(jnp.int32)

            def lookup(channel):
                return along(tables[0][channel], knot) + t * along(tables[1][channel], knot)

            lit = jnp.abs(gx * light0 + gy * light1 + gz * light2)
            lit = 0.3 + lit * lax.rsqrt(gx * gx + gy * gy + gz * gz + 4.0)
            inside = jnp.minimum(masks[here, 0:CZ], masks[here, CZ : 2 * CZ]) > 0.0
            tau = jnp.where(inside, lookup(3), 0.0)
            high = tau.astype(BF16)
            parts[here, 6 * CZ : 7 * CZ] = high
            parts[here, 7 * CZ : 8 * CZ] = (tau - high.astype(F32)).astype(BF16)
            for channel in range(3):
                colors[here, channel * CZ : (channel + 1) * CZ] = lookup(channel) * lit

    def depths(x, half):
        here = pl.ds(half * HALF, HALF)
        each[x][4][here, :] = matmul(each[x][3][here, 6 * CZ :], square_ref[0 : 2 * CZ, :])

    def weigh(x, chunk):
        _, _, colors, parts, sums, _ = each[x]
        for row in range(chunk * CHUNK, (chunk + 1) * CHUNK, WROWS):
            here = pl.ds(row, WROWS)
            weight = jnp.exp2(sums[here, 0:CZ]) - jnp.exp2(sums[here, CZ : 2 * CZ])
            for channel in range(3):
                value = weight * colors[here, channel * CZ : (channel + 1) * CZ]
                high = value.astype(BF16)
                parts[here, 2 * channel * CZ : (2 * channel + 1) * CZ] = high
                parts[here, (2 * channel + 1) * CZ : (2 * channel + 2) * CZ] = (
                    value - high.astype(F32)
                ).astype(BF16)

    def gathered(x, half):
        here = pl.ds(half * HALF, HALF)
        part = matmul(each[x][3][here, :], gather_ref[x])
        if x == cells[0]:
            total[here, :] = part if earlier is None else earlier[here, :] + part
        else:
            total[here, :] += part

    count = NY // CHUNK
    middle = count // 2
    for step in range(-1, len(cells) + 1):
        now = cells[step] if 0 <= step < len(cells) else None
        after = cells[step + 1] if step + 1 < len(cells) else None
        past = cells[step - 1] if step > 0 else None
        for chunk in range(count):
            if now is not None:
                classify(now, chunk)
            if after is not None:
                differences(after, chunk)
            if chunk >= middle and now is not None:
                weigh(now, chunk - middle)
            if chunk < middle and past is not None:
                weigh(past, chunk + middle)
            if chunk == middle - 1:
                if now is not None:
                    depths(now, 0)
                if past is not None:
                    gathered(past, 1)
                if after is not None:
                    resampled(after, 0)
            if chunk == middle + 1 and after is not None:
                resampled(after, 1)
        if now is not None:
            depths(now, 1)
            gathered(now, 0)
        if after is not None:
            resampled(after, 2)
            distances(after)


def compose(total, lower_ref, upper_ref):
    image = total[...].T
    depth = jnp.zeros((8, NY), F32)
    color = [jnp.zeros((8, NY), F32) for _ in range(3)]
    for group in range(CX):
        through = jnp.exp2(depth)
        for channel in range(3):
            at = (group * 4 + channel) * 8
            color[channel] = color[channel] + through * image[at : at + 8]
        at = (group * 4 + 3) * 8
        depth = depth + image[at : at + 8]
    planes = color + [depth]
    sub = iota((8, CZ), 0)
    lane = iota((8, CZ), 1)
    for m in range(NY // CZ):
        tile = [plane[:, m * CZ : (m + 1) * CZ] for plane in planes]
        turned = [pltpu.roll(part, 4, 0) for part in tile]
        for ref, a, b in (
            (lower_ref, jnp.where(sub < 4, tile[0], turned[1]), jnp.where(sub < 4, tile[2], turned[3])),
            (upper_ref, jnp.where(sub < 4, turned[0], tile[1]), jnp.where(sub < 4, turned[2], tile[3])),
        ):
            ref[2 * m] = jnp.where(lane < SHARE, a, pltpu.roll(b, SHARE, 1))
            ref[2 * m + 1] = jnp.where(lane < SHARE, pltpu.roll(a, SHARE, 1), b)


def buffers():
    return [
        pltpu.VMEM((2, NY, width * CZ), kind)
        for width, kind in ((4, BF16), (4, F32), (3, F32), (8, BF16), (2, F32), (2, F32))
    ]


def render_inner(*operands):
    return pl.pallas_call(
        inner_kernel,
        out_shape=jax.ShapeDtypeStruct((NY, CZ), F32),
        in_specs=[VMEM] * len(operands),
        out_specs=VMEM,
        scratch_shapes=buffers(),
        compiler_params=pltpu.CompilerParams(vmem_limit_bytes=LIMIT),
        name="inner",
        interpret=INTERPRET,
    )(*operands)


def render_outer(*operands):
    block = jax.ShapeDtypeStruct((8, 8, CZ), F32)
    return pl.pallas_call(
        outer_kernel,
        out_shape=(block, block),
        in_specs=[VMEM] * len(operands),
        out_specs=(VMEM, VMEM),
        scratch_shapes=[pltpu.VMEM((NY, CZ), F32)] + buffers(),
        compiler_params=pltpu.CompilerParams(vmem_limit_bytes=LIMIT),
        name="outer",
        interpret=INTERPRET,
    )(*operands)


def fold_kernel(pieces_ref, out_ref):
    sub = iota((8, CZ), 0)
    lane = iota((8, CZ), 1)
    color = jnp.zeros((8, CZ), F32)
    depth = jnp.zeros((8, CZ), F32)
    for d in range(pieces_ref.shape[0]):
        for side in range(2):
            piece = pieces_ref[d, side]
            own = jnp.where(lane >= SHARE, piece, pltpu.roll(piece, SHARE, 1))
            own = jnp.where(sub >= 4, own, pltpu.roll(own, 4, 0))
            color = color + jnp.exp2(depth) * piece
            depth = depth + own
    opacity = 1.0 - jnp.exp2(depth)
    color = jnp.where((sub >= 4) & (lane >= SHARE), opacity, color)
    turned = pltpu.roll(color, SHARE, 1)
    out_ref[0] = color[0:4, 0:SHARE]
    out_ref[1] = color[4:8, 0:SHARE]
    out_ref[2] = turned[0:4, 0:SHARE]
    out_ref[3] = turned[4:8, 0:SHARE]


def fold(pieces):
    return pl.pallas_call(
        fold_kernel,
        out_shape=jax.ShapeDtypeStruct((4, CX, SHARE), F32),
        in_specs=[VMEM],
        out_specs=VMEM,
        compiler_params=pltpu.CompilerParams(vmem_limit_bytes=LIMIT),
        name="fold",
        interpret=INTERPRET,
    )(pieces)


def body(volume, resample, transfer, light, ray_bounds):
    planes = lax.axis_size("plane")
    depths = lax.axis_size("depth")

    def exchanged(value, axis, first):
        pairs = []
        for i in range(first, lax.axis_size(axis) - 1, 2):
            pairs += [(i, i + 1), (i + 1, i)]
        return lax.ppermute(value, axis, pairs)

    odd = lax.axis_index("plane") % 2
    outward = lax.dynamic_index_in_dim(volume, (CX - 1) * (1 - odd), 0, keepdims=False)
    inward = lax.dynamic_index_in_dim(volume, (CX - 1) * odd, 0, keepdims=False)
    plane_even = exchanged(outward, "plane", 0)
    plane_odd = exchanged(inward, "plane", 1)
    faces = pack_faces(volume)
    depth_even = exchanged(faces, "depth", 0)
    depth_odd = exchanged(faces, "depth", 1)
    tables, limits = prepare(transfer, light, ray_bounds)
    shared = (resample, tables, limits, *constants())
    inner = render_inner(volume, depth_even, depth_odd, *shared)
    lower, upper = render_outer(
        volume, plane_even, plane_odd, depth_even, depth_odd, *shared, inner
    )

    def skewed(value, extra):
        pairs = [
            (p * depths + d, (p + d + extra) * depths + d)
            for p in range(planes)
            for d in range(depths)
            if p + d + extra < planes
        ]
        return lax.ppermute(value, ("plane", "depth"), pairs)

    pieces = jnp.stack([skewed(lower, 0), skewed(upper, 1)], axis=1)
    pieces = lax.all_to_all(pieces, "depth", 0, 0, tiled=True)
    return fold(pieces)


def solution(mesh):
    in_specs = (P("plane", None, "depth"), P(), P(), P(), P())
    out_specs = P(None, "plane", "depth")
    return jax.shard_map(body, mesh=mesh, in_specs=in_specs, out_specs=out_specs, check_vma=False)
```

```python
import functools
import math

import jax
import jax.numpy as jnp
import numpy as np
from jax import lax
from jax.experimental import pallas as pl
from jax.experimental.pallas import tpu as pltpu
from jax.sharding import PartitionSpec as P

INTERPRET = False
F32 = jnp.float32
BF16 = jnp.bfloat16
VMEM = pl.BlockSpec(memory_space=pltpu.VMEM)
SMEM = pl.BlockSpec(memory_space=pltpu.SMEM)

CX, NY, CZ, KNOTS, SHARE = 4, 512, 128, 16, 64
GROUP = CZ // CX
CHUNK = 64
WROWS = 16
HALF = 256
LIMIT = 14 << 20
INNER, OUTER = (1, 2), (0, 3)


def matmul(a, b):
    return jnp.dot(a, b, preferred_element_type=F32)


def along(table, index):
    numbers = lax.GatherDimensionNumbers(
        offset_dims=(),
        collapsed_slice_dims=(1,),
        start_index_map=(1,),
        operand_batching_dims=(0,),
        start_indices_batching_dims=(0,),
    )
    mode = lax.GatherScatterMode.PROMISE_IN_BOUNDS
    return lax.gather(table, index[..., None], numbers, slice_sizes=(1, 1), mode=mode)


def iota(shape, dim):
    return lax.broadcasted_iota(jnp.int32, shape, dim)


def faces_kernel(vol_ref, out_ref):
    lane = iota((8, CZ), 1)
    for x in range(CX):
        packed = jnp.zeros((8, CZ), F32)
        for j in range(NY // 8):
            row = vol_ref[x, 8 * j : 8 * j + 8, :]
            moved = pltpu.roll(row, 2 * j, 1) if j else row
            keep = (lane == 2 * j) | (lane == (2 * j - 1) % CZ)
            packed = jnp.where(keep, moved, packed)
        out_ref[x] = packed


def pack_faces(volume):
    return pl.pallas_call(
        faces_kernel,
        out_shape=jax.ShapeDtypeStruct((CX, 8, CZ), F32),
        in_specs=[VMEM],
        out_specs=VMEM,
        compiler_params=pltpu.CompilerParams(vmem_limit_bytes=LIMIT),
        name="faces",
        interpret=INTERPRET,
    )(volume)


def prepare_kernel(
    transfer_ref, light_ref, bounds_ref, tables_ref, limits_ref, window, square, sem
):
    planes = bounds_ref.shape[1] // CX
    column = CX * (lax.axis_index("plane") + lax.axis_index("depth"))
    start = pl.multiple_of(jnp.minimum((column // 8) * 8, planes * CX - 16), 8)
    copy = pltpu.make_async_copy(bounds_ref.at[:, pl.ds(start, 16), :], window, sem)
    copy.start()
    lane = iota((8, CZ), 1)
    square[...] = jnp.zeros_like(square)
    square[0:4, 0:KNOTS] = transfer_ref[...]
    knots = square[...]
    step = jnp.where(lane < KNOTS - 1, pltpu.roll(knots, CZ - 1, 1) - knots, 0.0)
    scale = jnp.where(iota((8, CZ), 0) == 3, -(2.0 / 1024) * math.log2(math.e), 1.0)
    tables_ref[0] = (knots - lane.astype(F32) * step) * scale
    tables_ref[1] = step * scale
    tables_ref[2] = jnp.zeros((8, CZ), F32)
    for axis in range(3):
        tables_ref[2, axis : axis + 1] = jnp.broadcast_to(light_ref[axis] * 0.7, (1, CZ))
    copy.wait()
    base = lax.axis_index("depth") * CZ
    turn = 16 - jnp.minimum(column - start, 15)
    ends = jnp.clip(window[...] - base, 0, CZ).astype(F32)
    first = pltpu.roll(ends[0], turn, 0)[0:8]
    last = pltpu.roll(ends[1], turn, 0)[0:8]
    limits = jnp.concatenate(
        [first, last, jnp.ones((1, NY), F32), jnp.zeros((CZ - 17, NY), F32)], axis=0
    )
    limits_ref[...] = limits.T.astype(BF16)


def prepare(transfer, light, ray_bounds):
    return pl.pallas_call(
        prepare_kernel,
        out_shape=(
            jax.ShapeDtypeStruct((3, 8, CZ), F32),
            jax.ShapeDtypeStruct((NY, CZ), BF16),
        ),
        in_specs=[VMEM, SMEM, pl.BlockSpec(memory_space=pltpu.HBM)],
        out_specs=(VMEM, VMEM),
        scratch_shapes=[
            pltpu.VMEM((2, 16, NY), jnp.int32),
            pltpu.VMEM((8, CZ), F32),
            pltpu.SemaphoreType.DMA,
        ],
        compiler_params=pltpu.CompilerParams(vmem_limit_bytes=LIMIT),
        name="prepare",
        interpret=INTERPRET,
    )(transfer.T, light, pltpu.with_memory_space_constraint(ray_bounds, pltpu.HBM))


def constants():
    src = np.arange(2 * CZ)[:, None] % CZ
    lane = np.arange(2 * CZ)[None, :]
    dst = lane % CZ
    before = (src < dst) | ((src == dst) & (lane >= CZ))
    prefix = (src // GROUP == dst // GROUP) & before
    row = np.arange(CZ)[None, :, None]
    z = np.arange(CZ)[None, None, :]
    pixel = np.arange(CX)[:, None, None] + z // GROUP
    ahead = np.where(row == pixel, -1.0, np.where(row == 16, z + 0.5, 0.0))
    behind = np.where(row == pixel + 8, 1.0, np.where(row == 16, -(z + 0.5), 0.0))
    select = np.concatenate([ahead, behind], axis=2)
    row = np.arange(8 * CZ)[None, :, None]
    group = (row % CZ) // GROUP
    place = (group * 4 + row // (2 * CZ)) * 8 + np.arange(CX)[:, None, None] + group
    gather = np.arange(CZ)[None, None, :] == place
    square = np.concatenate([prefix, select.reshape(CX * CZ, 2 * CZ)], axis=0)
    return [jnp.asarray(np.asarray(a, np.float32), BF16) for a in (square, gather)]


def inner_kernel(
    vol_ref, depth_even_ref, depth_odd_ref, resample_ref, tables_ref, limits_ref,
    square_ref, gather_ref,
    total_ref, *buffers,
):
    accumulate(
        INNER, vol_ref, None, None, depth_even_ref, depth_odd_ref,
        resample_ref, tables_ref, limits_ref, square_ref, gather_ref,
        None, total_ref, buffers,
    )


def outer_kernel(
    vol_ref, plane_even_ref, plane_odd_ref, depth_even_ref, depth_odd_ref,
    resample_ref, tables_ref, limits_ref, square_ref, gather_ref, inner_ref,
    upper_ref, lower_ref, total, *buffers,
):
    accumulate(
        OUTER, vol_ref, plane_even_ref, plane_odd_ref, depth_even_ref, depth_odd_ref,
        resample_ref, tables_ref, limits_ref, square_ref, gather_ref,
        inner_ref, total, buffers,
    )
    compose(total, lower_ref, upper_ref)


def accumulate(
    cells, vol_ref, plane_even_ref, plane_odd_ref, depth_even_ref, depth_odd_ref,
    resample_ref, tables_ref, limits_ref, square_ref, gather_ref,
    earlier, total, buffers,
):
    lane8 = iota((8, CZ), 1)
    tables = [
        [jnp.broadcast_to(tables_ref[i, c : c + 1], (8, CZ)) for c in range(4)] for i in range(2)
    ]
    light0, light1, light2 = (
        jnp.broadcast_to(tables_ref[2, c : c + 1], (8, CZ)) for c in range(3)
    )
    plane_odd = lax.axis_index("plane") % 2 == 1
    depth_odd = lax.axis_index("depth") % 2 == 1
    lane = iota((CHUNK, CZ), 1)
    each = {x: [buffer.at[i] for buffer in buffers] for i, x in enumerate(cells)}
    packed = {
        x: jnp.where(
            lane8 % 2 == 0,
            pltpu.roll(jnp.where(depth_odd, depth_even_ref[x], depth_odd_ref[x]), 1, 1),
            pltpu.roll(jnp.where(depth_odd, depth_odd_ref[x], depth_even_ref[x]), CZ - 1, 1),
        )
        for x in cells
    }

    def beside(x, here):
        if x < 0:
            return jnp.where(plane_odd, plane_even_ref[here, :], plane_odd_ref[here, :])
        if x == CX:
            return jnp.where(plane_odd, plane_odd_ref[here, :], plane_even_ref[here, :])
        return vol_ref[x, here, :]

    def differences(x, chunk):
        fields = each[x][0]
        r0 = chunk * CHUNK
        here = pl.ds(r0, CHUNK)
        f = vol_ref[x, here, :]
        below = beside(x - 1, here)
        above = beside(x + 1, here)
        blank = jnp.zeros((1, CZ), F32)
        if r0 == 0:
            prev = jnp.concatenate([blank, vol_ref[x, 0 : CHUNK - 1, :]], axis=0)
        else:
            prev = vol_ref[x, r0 - 1 : r0 + CHUNK - 1, :]
        if r0 + CHUNK == NY:
            following = jnp.concatenate([vol_ref[x, r0 + 1 : NY, :], blank], axis=0)
        else:
            following = vol_ref[x, r0 + 1 : r0 + CHUNK + 1, :]
        ends = jnp.concatenate(
            [
                pltpu.roll(packed[x], (CZ - 2 * j) % CZ, 1) if j else packed[x]
                for j in range(r0 // 8, (r0 + CHUNK) // 8)
            ],
            axis=0,
        )
        front = jnp.where(lane == 0, ends, pltpu.roll(f, 1, 1))
        back = jnp.where(lane == CZ - 1, ends, pltpu.roll(f, CZ - 1, 1))
        fields[here, 0:CZ] = f.astype(BF16)
        fields[here, CZ : 2 * CZ] = (above - below).astype(BF16)
        fields[here, 2 * CZ : 3 * CZ] = (following - prev).astype(BF16)
        fields[here, 3 * CZ : 4 * CZ] = (back - front).astype(BF16)

    def resampled(x, window):
        fields, samples = each[x][:2]
        first, last, k0 = ((0, 192, 0), (192, 320, 128), (320, 512, 256))[window]
        samples[first:last, :] = matmul(
            resample_ref[first:last, k0 : k0 + 256], fields[k0 : k0 + 256, :]
        )

    def distances(x):
        each[x][5][...] = matmul(limits_ref[...], square_ref[(2 + x) * CZ : (3 + x) * CZ, :])

    def classify(x, chunk):
        _, samples, colors, parts, _, masks = each[x]
        for row in range(chunk * CHUNK, (chunk + 1) * CHUNK, 8):
            here = pl.ds(row, 8)
            d = samples[here, 0:CZ]
            gx = samples[here, CZ : 2 * CZ]
            gy = samples[here, 2 * CZ : 3 * CZ]
            gz = samples[here, 3 * CZ : 4 * CZ]
            t = jnp.clip(d * 3.0 + 7.5, 0.0, KNOTS - 1.0)
            knot = t.astype(jnp.int32)

            def lookup(channel):
                return along(tables[0][channel], knot) + t * along(tables[1][channel], knot)

            lit = jnp.abs(gx * light0 + gy * light1 + gz * light2)
            lit = 0.3 + lit * lax.rsqrt(gx * gx + gy * gy + gz * gz + 4.0)
            inside = jnp.minimum(masks[here, 0:CZ], masks[here, CZ : 2 * CZ]) > 0.0
            tau = jnp.where(inside, lookup(3), 0.0)
            high = tau.astype(BF16)
            parts[here, 6 * CZ : 7 * CZ] = high
            parts[here, 7 * CZ : 8 * CZ] = (tau - high.astype(F32)).astype(BF16)
            for channel in range(3):
                colors[here, channel * CZ : (channel + 1) * CZ] = lookup(channel) * lit

    def depths(x, half):
        here = pl.ds(half * HALF, HALF)
        each[x][4][here, :] = matmul(each[x][3][here, 6 * CZ :], square_ref[0 : 2 * CZ, :])

    def weigh(x, chunk):
        _, _, colors, parts, sums, _ = each[x]
        for row in range(chunk * CHUNK, (chunk + 1) * CHUNK, WROWS):
            here = pl.ds(row, WROWS)
            weight = jnp.exp2(sums[here, 0:CZ]) - jnp.exp2(sums[here, CZ : 2 * CZ])
            for channel in range(3):
                value = weight * colors[here, channel * CZ : (channel + 1) * CZ]
                high = value.astype(BF16)
                parts[here, 2 * channel * CZ : (2 * channel + 1) * CZ] = high
                parts[here, (2 * channel + 1) * CZ : (2 * channel + 2) * CZ] = (
                    value - high.astype(F32)
                ).astype(BF16)

    def gathered(x, half):
        here = pl.ds(half * HALF, HALF)
        part = matmul(each[x][3][here, :], gather_ref[x])
        if x == cells[0]:
            total[here, :] = part if earlier is None else earlier[here, :] + part
        else:
            total[here, :] += part

    count = NY // CHUNK
    middle = count // 2
    for step in range(-1, len(cells) + 1):
        now = cells[step] if 0 <= step < len(cells) else None
        after = cells[step + 1] if step + 1 < len(cells) else None
        past = cells[step - 1] if step > 0 else None
        for chunk in range(count):
            if now is not None:
                classify(now, chunk)
            if after is not None:
                differences(after, chunk)
            if chunk >= middle and now is not None:
                weigh(now, chunk - middle)
            if chunk < middle and past is not None:
                weigh(past, chunk + middle)
            if chunk == middle - 1:
                if now is not None:
                    depths(now, 0)
                if past is not None:
                    gathered(past, 1)
                if after is not None:
                    resampled(after, 0)
            if chunk == middle + 1 and after is not None:
                resampled(after, 1)
        if now is not None:
            depths(now, 1)
            gathered(now, 0)
        if after is not None:
            resampled(after, 2)
            distances(after)


def compose(total, lower_ref, upper_ref):
    image = total[...].T
    depth = jnp.zeros((8, NY), F32)
    color = [jnp.zeros((8, NY), F32) for _ in range(3)]
    for group in range(CX):
        through = jnp.exp2(depth)
        for channel in range(3):
            at = (group * 4 + channel) * 8
            color[channel] = color[channel] + through * image[at : at + 8]
        at = (group * 4 + 3) * 8
        depth = depth + image[at : at + 8]
    planes = color + [depth]
    sub = iota((8, CZ), 0)
    lane = iota((8, CZ), 1)
    for m in range(NY // CZ):
        tile = [plane[:, m * CZ : (m + 1) * CZ] for plane in planes]
        turned = [pltpu.roll(part, 4, 0) for part in tile]
        for ref, a, b in (
            (lower_ref, jnp.where(sub < 4, tile[0], turned[1]), jnp.where(sub < 4, tile[2], turned[3])),
            (upper_ref, jnp.where(sub < 4, turned[0], tile[1]), jnp.where(sub < 4, turned[2], tile[3])),
        ):
            ref[2 * m] = jnp.where(lane < SHARE, a, pltpu.roll(b, SHARE, 1))
            ref[2 * m + 1] = jnp.where(lane < SHARE, pltpu.roll(a, SHARE, 1), b)


def buffers():
    return [
        pltpu.VMEM((2, NY, width * CZ), kind)
        for width, kind in ((4, BF16), (4, F32), (3, F32), (8, BF16), (2, F32), (2, F32))
    ]


def render_inner(*operands):
    return pl.pallas_call(
        inner_kernel,
        out_shape=jax.ShapeDtypeStruct((NY, CZ), F32),
        in_specs=[VMEM] * len(operands),
        out_specs=VMEM,
        scratch_shapes=buffers(),
        compiler_params=pltpu.CompilerParams(vmem_limit_bytes=LIMIT),
        name="inner",
        interpret=INTERPRET,
    )(*operands)


def render_outer(*operands):
    block = jax.ShapeDtypeStruct((8, 8, CZ), F32)
    return pl.pallas_call(
        outer_kernel,
        out_shape=(block, block),
        in_specs=[VMEM] * len(operands),
        out_specs=(VMEM, VMEM),
        scratch_shapes=[pltpu.VMEM((NY, CZ), F32)] + buffers(),
        compiler_params=pltpu.CompilerParams(vmem_limit_bytes=LIMIT),
        name="outer",
        interpret=INTERPRET,
    )(*operands)


def fold_kernel(pieces_ref, out_ref):
    sub = iota((8, CZ), 0)
    lane = iota((8, CZ), 1)
    color = jnp.zeros((8, CZ), F32)
    depth = jnp.zeros((8, CZ), F32)
    for d in range(pieces_ref.shape[0]):
        for side in (1, 0):
            piece = pieces_ref[d, side]
            own = jnp.where(lane >= SHARE, piece, pltpu.roll(piece, SHARE, 1))
            own = jnp.where(sub >= 4, own, pltpu.roll(own, 4, 0))
            color = color + jnp.exp2(depth) * piece
            depth = depth + own
    opacity = 1.0 - jnp.exp2(depth)
    color = jnp.where((sub >= 4) & (lane >= SHARE), opacity, color)
    turned = pltpu.roll(color, SHARE, 1)
    out_ref[0] = color[0:4, 0:SHARE]
    out_ref[1] = color[4:8, 0:SHARE]
    out_ref[2] = turned[0:4, 0:SHARE]
    out_ref[3] = turned[4:8, 0:SHARE]


def fold(pieces):
    return pl.pallas_call(
        fold_kernel,
        out_shape=jax.ShapeDtypeStruct((4, CX, SHARE), F32),
        in_specs=[VMEM],
        out_specs=VMEM,
        compiler_params=pltpu.CompilerParams(vmem_limit_bytes=LIMIT),
        name="fold",
        interpret=INTERPRET,
    )(pieces)


def body(volume, resample, transfer, light, ray_bounds):
    planes = lax.axis_size("plane")
    depths = lax.axis_size("depth")

    def exchanged(value, axis, first):
        pairs = []
        for i in range(first, lax.axis_size(axis) - 1, 2):
            pairs += [(i, i + 1), (i + 1, i)]
        return lax.ppermute(value, axis, pairs)

    odd = lax.axis_index("plane") % 2
    outward = lax.dynamic_index_in_dim(volume, (CX - 1) * (1 - odd), 0, keepdims=False)
    inward = lax.dynamic_index_in_dim(volume, (CX - 1) * odd, 0, keepdims=False)
    plane_even = exchanged(outward, "plane", 0)
    plane_odd = exchanged(inward, "plane", 1)
    faces = pack_faces(volume)
    depth_even = exchanged(faces, "depth", 0)
    depth_odd = exchanged(faces, "depth", 1)
    tables, limits = prepare(transfer, light, ray_bounds)
    shared = (resample, tables, limits, *constants())
    inner = render_inner(volume, depth_even, depth_odd, *shared)
    upper, lower = render_outer(
        volume, plane_even, plane_odd, depth_even, depth_odd, *shared, inner
    )

    def skewed(value, extra):
        pairs = [
            (p * depths + d, (p + d + extra) * depths + d)
            for p in range(planes)
            for d in range(depths)
            if p + d + extra < planes
        ]
        return lax.ppermute(value, ("plane", "depth"), pairs)

    right = skewed(upper, 1)
    left = skewed(lower, 0)
    pieces = jnp.stack([right, left], axis=1)
    pieces = lax.all_to_all(pieces, "depth", 0, 0, tiled=True)
    return fold(pieces)


def solution(mesh):
    in_specs = (P("plane", None, "depth"), P(), P(), P(), P())
    out_specs = P(None, "plane", "depth")
    return jax.shard_map(body, mesh=mesh, in_specs=in_specs, out_specs=out_specs, check_vma=False)
```
